32 devices in a mesh: grp: 4 (over y, core), span: 8 (over z, x).
Axes of the slice: x: 2, y: 2, z: 4, core: 2. Of those that a mesh axis runs over, the one named last changes fastest.
Arguments:
- record: float32 [131072, 128], P(('grp', 'span')), may hold values from -96 to 96, as said below
Outputs:
- triangle: float32 [512, 512], replicated
- operator: float32 [512, 512], replicated
The draws below stay inside these ranges and needn't reach their ends.
Inputs may be any that keep to these rules, and one draw needn't show every extreme that they name: `record`: Real-valued probe samples.
All inputs are finite; a program needn't handle non-finite values.
Results may differ from the reference program's by a relative error of at most 0.0003.
Values sent between devices are 32-bit elements; how exact they have to be, the bound alone decides.
A program may use at most 64 MiB of HBM per device.

```python
import jax
import jax.numpy as jnp
from jax import lax

COMPS = 128
LAGS = 4
DELAY = 1024
ROWS_DEV = 4096
COLS = 512
SAMPLES = 131072
HROWS = 127999


def draw_record(key, part):
    keys = jax.random.split(jax.random.fold_in(key, 17), 5)
    colscale = jnp.exp(jax.random.uniform(keys[0], (1, COMPS), jnp.float32) * 2.302585)
    freq = jax.random.randint(keys[1], (1, COMPS), 1, 32768)
    phase = jax.random.randint(keys[2], (1, COMPS), 0, 65536)
    times = jnp.arange(SAMPLES, dtype=jnp.int32)[:, None]
    turns = (freq * (times % 65536) + phase) % 65536
    wave = 0.8 * jnp.sin(turns.astype(jnp.float32) * (6.2831853 / 65536.0))
    envelope = 0.6 + 1.2 * times.astype(jnp.float32) / SAMPLES
    noise = jax.random.truncated_normal(keys[4], -4.0, 4.0, (SAMPLES, COMPS), jnp.float32)
    return (colscale * envelope * (noise + wave)).astype(jnp.float32)


def setup_inputs(seed: int = 0) -> dict:
    streams_of = jax.random.split(jax.random.key(seed), 2)
    return {
        "record": draw_record(jax.random.fold_in(streams_of[1], 71), 0),
    }


def block_terms(padded, start, count):
    lead = (LAGS - 1) * DELAY + 1
    ext = lax.dynamic_slice_in_dim(padded, start, count + lead, 0)
    hank = jnp.concatenate([ext[k * DELAY:k * DELAY + count + 1] for k in range(LAGS)], 1)
    times = start + jnp.arange(count, dtype=jnp.int32)
    weight = jnp.where(times < HROWS, 1.0, 0.0) - 0.5 * jnp.where(times == 0, 1.0, 0.0) - 0.5 * jnp.where(times == HROWS, 1.0, 0.0)
    weight = weight.astype(jnp.float32)
    inside = jnp.where(times < HROWS, 1.0, 0.0).astype(jnp.float32)
    head = hank[:count]
    gram = lax.dot_general((head * weight[:, None]).astype(jnp.float32), head.astype(jnp.float32), (((0,), (0,)), ((), ())), precision=lax.Precision.HIGHEST, preferred_element_type=jnp.float32)
    cross = lax.dot_general((head * inside[:, None]).astype(jnp.float32), hank[1:count + 1].astype(jnp.float32), (((0,), (0,)), ((), ())), precision=lax.Precision.HIGHEST, preferred_element_type=jnp.float32)
    return (gram, cross)

def reference(record):
    lead = (LAGS - 1) * DELAY + 1
    padded = jnp.concatenate([record, jnp.zeros((lead, COMPS), jnp.float32)], 0)
    blocks = SAMPLES // ROWS_DEV

    def step(carry, index):
        gram, cross = block_terms(padded, (index * ROWS_DEV).astype(jnp.int32), ROWS_DEV)
        return ((carry[0] + gram, carry[1] + cross), None)
    zeros = jnp.zeros((COLS, COLS), jnp.float32)
    (gram, cross), unused = lax.scan(step, (zeros, zeros), jnp.arange(blocks, dtype=jnp.int32))
    lower = jnp.linalg.cholesky(gram / HROWS)
    middle = jax.scipy.linalg.solve_triangular(lower, cross / HROWS, lower=True)
    operator = jax.scipy.linalg.solve_triangular(lower, middle.T, lower=True).T
    return (lower.T, operator)
```

```python
import functools

import jax
import jax.numpy as jnp
from jax import lax
from jax.experimental import pallas as pl
from jax.experimental.pallas import tpu as pltpu
from jax.sharding import PartitionSpec as P

LAGS = 4
DELAY = 1024
AXES = ("grp", "span")
HIGH = lax.Precision.HIGHEST
MESH = pl.DeviceIdType.MESH
UNIT = 128
HALF = DELAY // 2
CHUNKS = HALF // UNIT
GRAM = [(k, l) for k in range(LAGS) for l in range(k, LAGS)]
CROSS = [(k, l) for k in range(LAGS) for l in range(LAGS)]
NB = len(GRAM) + len(CROSS)


def contract(left, right, dims, precision=None):
    return lax.dot_general(
        left, right, (dims, ((), ())), precision=precision,
        preferred_element_type=jnp.float32,
    )


def factor(block):
    n = block.shape[0]
    groups = n // 8
    lane = lax.broadcasted_iota(jnp.int32, (8, n), 1)
    sub = lax.broadcasted_iota(jnp.int32, (8, n), 0)
    a = [block[8 * g:8 * g + 8, :] for g in range(groups)]
    b = [jnp.where(lane == sub + 8 * g, 1.0, 0.0) for g in range(groups)]
    for k in range(n):
        g, r = divmod(k, 8)
        inverse = 1.0 / a[g][r:r + 1, k:k + 1]
        row = a[g][r:r + 1, :] * inverse
        brow = b[g][r:r + 1, :] * inverse
        for h in range(g, groups):
            if h == g and r == 7:
                continue
            column = jnp.broadcast_to(a[h][:, k:k + 1], (8, n))
            if h == g:
                column = jnp.where(sub > r, column, 0.0)
            a[h] = a[h] - column * row
            b[h] = b[h] - column * brow
    for g in range(groups):
        here = lane == sub + 8 * g
        pivot = jnp.sum(jnp.where(here, a[g], 0.0), axis=1, keepdims=True)
        scale = 1.0 / jnp.sqrt(pivot)
        a[g] = jnp.where(lane >= sub + 8 * g, a[g] * scale, 0.0)
        b[g] = b[g] * scale
    return jnp.concatenate(a, 0), jnp.concatenate(b, 0)


def solve_kernel(comps, scale, sums_ref, tri_ref, op_ref, work, inverses):
    size = LAGS * comps
    for i in range(LAGS):
        rows = pl.ds(i * comps, comps)
        for j in range(LAGS):
            if j >= i:
                at = GRAM.index((i, j)) * comps
                work[i, :, pl.ds(j * comps, comps)] = sums_ref[pl.ds(at, comps), :] * scale
            at = (len(GRAM) + CROSS.index((i, j))) * comps
            work[i, :, pl.ds(size + j * comps, comps)] = sums_ref[pl.ds(at, comps), :] * scale
        if i:
            work[i, :, pl.ds(0, i * comps)] = jnp.zeros((comps, i * comps), jnp.float32)
            tri_ref[rows, pl.ds(0, i * comps)] = jnp.zeros((comps, i * comps), jnp.float32)

    def step(i, carry):
        at = pl.multiple_of(i * comps, comps)
        upper, inverse = factor(work[i, :, pl.ds(at, comps)])
        inverses[i] = inverse
        work[i] = contract(inverse, work[i], ((1,), (0,)), HIGH)
        work[i, :, pl.ds(at, comps)] = upper

        def update(j, carry):
            to = pl.multiple_of(j * comps, comps)
            work[j] = work[j] - contract(work[i, :, pl.ds(to, comps)], work[i], ((0,), (0,)), HIGH)
            return carry
        lax.fori_loop(i + 1, LAGS, update, 0)
        return carry
    lax.fori_loop(0, LAGS, step, 0)

    for i in range(LAGS):
        for j in range(i, LAGS):
            tri_ref[pl.ds(i * comps, comps), pl.ds(j * comps, comps)] = work[i, :, pl.ds(j * comps, comps)]
    for b in range(LAGS):
        rest = jnp.concatenate(
            [work[i, :, pl.ds((LAGS + b) * comps, comps)] for i in range(LAGS)], 0)
        if b:
            rest = rest - contract(
                op_ref[:, pl.ds(0, b * comps)],
                tri_ref[pl.ds(0, b * comps), pl.ds(b * comps, comps)], ((1,), (0,)), HIGH)
        op_ref[:, pl.ds(b * comps, comps)] = contract(rest, inverses[b], ((1,), (1,)), HIGH)


def halves(x):
    spread = x * 65537.0
    high = spread - (spread - x)
    return high.astype(jnp.bfloat16), (x - high).astype(jnp.bfloat16)


def quarters(x):
    n = x.shape[0] // 2
    return (x[:n, :n] + x[:n, n:]) + (x[n:, :n] + x[n:, n:])


def prepare(window, at, left, right, after):
    cols = pl.ds(at, UNIT)
    rows = window[:UNIT]
    high, low = halves(rows)
    right[cols, pl.ds(0, UNIT)] = high
    right[cols, pl.ds(UNIT, UNIT)] = low
    high, low = halves(rows.T)
    left[pl.ds(0, UNIT), cols] = high
    left[pl.ds(UNIT, UNIT), cols] = low
    high, low = halves(pltpu.roll(window, window.shape[0] - 1, 0)[:UNIT])
    after[cols, pl.ds(0, UNIT)] = high
    after[cols, pl.ds(UNIT, UNIT)] = low


def product(left, lcol, right, rrow, depth):
    lcol = pl.multiple_of(lcol, UNIT)
    rrow = pl.multiple_of(rrow, UNIT)
    return jnp.dot(left[:, pl.ds(lcol, depth)], right[pl.ds(rrow, depth), :],
                   preferred_element_type=jnp.float32)


def sums_kernel(groups, spans, piece, rec, out, ext, own, left, right, after, acc,
                eleft, eright, eafter, dgram, dcross, wgram, wcross, buf, slot_a, slot_b, slot_c,
                local_sem, xs, xr, zs, zr, es, er, as_, ar, bs, br, cs, cr, gcs, gcr, gbs, gbr, gas, gar):
    grp, span = lax.axis_index("grp"), lax.axis_index("span")
    pairs = spans // 2
    h, q = span % 2, span // 2
    core, y = grp % 2, grp // 2
    plane, place = groups, y * 2 + h
    at, count = grp * pairs + q, groups * pairs
    has_prev, has_next = at > 0, at < count - 1

    def device(pair, side):
        pair = (pair + count) % count
        return (pair // pairs, (pair % pairs) * 2 + side)

    def plane_peer(d):
        there = (place + d) % plane
        return ((there // 2) * 2 + core, q * 2 + there % 2)

    def line_peer(d):
        return (grp, ((q + d) % pairs) * 2 + h)

    core_peer = (y * 2 + 1 - core, span)
    partner = (grp, q * 2 + 1 - h)
    z_to = device(at - 1 + 2 * h, h)
    sends_z = jnp.where(h == 0, at, count - 1 - at) > 0
    gets_z = jnp.where(h == 0, count - 1 - at, at) > 0

    own_copy = pltpu.make_async_copy(
        rec.at[:, pl.ds(h * HALF, HALF), :], ext.at[pl.ds(1 + 7 * h, 4), pl.ds(0, HALF), :], local_sem.at[0])
    own_extra = pltpu.make_async_copy(
        rec.at[:, pl.ds((1 - h) * HALF, 8), :], ext.at[pl.ds(1 + 6 * h, 4), pl.ds(HALF, 8), :], local_sem.at[1])
    own_copy.start()
    own_extra.start()
    edge = (at * 2 + h == 0) | (at * 2 + h == 2 * count - 1)
    full_copy = pltpu.make_async_copy(rec, own.at[pl.ds(0, LAGS)], local_sem.at[2])

    @pl.when(edge)
    def _():
        full_copy.start()

    barrier = pltpu.get_barrier_semaphore()

    def greet(to):
        pl.semaphore_signal(barrier, inc=1, device_id=to, device_id_type=MESH)

    greet(core_peer)
    for d in range(1, plane):
        greet(plane_peer(d))
    for d in range(1, pairs):
        greet(line_peer(d))

    @pl.when(has_prev)
    def _():
        greet(device(at - 1, h))

    @pl.when(has_next)
    def _():
        greet(device(at + 1, h))

    @pl.when((h == 0) & has_prev)
    def _():
        greet(device(at - 1, 1))

    @pl.when((h == 1) & has_next)
    def _():
        greet(device(at + 1, 0))

    pl.semaphore_wait(
        barrier, plane + pairs - 1
        + jnp.where(has_prev, 1, 0) + jnp.where(has_next, 1, 0)
        + jnp.where((h == 0) & has_prev, 1, 0) + jnp.where((h == 1) & has_next, 1, 0))

    def remote(src, dst, send, recv, to):
        return pltpu.make_async_remote_copy(
            src_ref=src, dst_ref=dst, send_sem=send, recv_sem=recv, device_id=to, device_id_type=MESH)

    def x_copy(c):
        return remote(
            rec.at[:, pl.ds((1 - h) * HALF + c * UNIT, UNIT), :],
            ext.at[pl.ds(4 + h, 4), pl.ds(c * UNIT, UNIT), :], xs.at[c], xr.at[c], partner)

    def z_copy(c):
        return remote(
            rec.at[pl.ds(h, 3), pl.ds(h * HALF + c * UNIT, UNIT), :],
            ext.at[pl.ds(9 - 8 * h, 3), pl.ds(c * UNIT, UNIT), :], zs.at[c], zr.at[c], z_to)

    x_extra = remote(
        rec.at[:, pl.ds(h * HALF, 8), :], ext.at[pl.ds(3 + 2 * h, 4), pl.ds(HALF, 8), :],
        es.at[0], er.at[0], partner)
    z_extra = remote(
        rec.at[pl.ds(h, 3), pl.ds((1 - h) * HALF, 8), :], ext.at[pl.ds(9 - 9 * h, 3), pl.ds(HALF, 8), :],
        es.at[1], er.at[1], z_to)
    d_extra = remote(
        rec.at[pl.ds(0, 1), pl.ds(0, 8), :], ext.at[pl.ds(11, 1), pl.ds(HALF, 8), :],
        es.at[2], er.at[2], device(at - 1, 1))

    x_extra.start()
    for c in reversed(range(CHUNKS)):
        x_copy(c).start()

    @pl.when(sends_z)
    def _():
        z_extra.start()
        for c in reversed(range(CHUNKS)):
            z_copy(c).start()

    @pl.when((h == 0) & has_prev)
    def _():
        d_extra.start()

    @pl.when(jnp.logical_not(gets_z))
    def _():
        ext[pl.ds(9 - 8 * h, 3), pl.ds(0, HALF), :] = jnp.zeros((3, HALF, UNIT), jnp.float32)

    acc[...] = jnp.zeros(acc.shape, jnp.float32)

    @pl.when(edge)
    def _():
        last = jnp.where(at > 0, 1, 0)
        own[LAGS, pl.ds(0, 8), :] = jnp.zeros((8, UNIT), jnp.float32)
        full_copy.wait()
        parts = DELAY // UNIT

        def unit(t, carry):
            block, row = t // parts, (t % parts) * UNIT
            rows = own[last + block, pl.ds(pl.multiple_of(row, UNIT), UNIT), :]
            more = t + 1
            tail = own[last + more // parts, pl.ds(pl.multiple_of((more % parts) * UNIT, UNIT), 8), :]
            prepare(jnp.concatenate([rows, tail], 0), pl.multiple_of(t * UNIT, UNIT), eleft, eright, eafter)
            return carry
        lax.fori_loop(0, 3 * parts, unit, 0)

        def excess(t, carry):
            i, j = t // 3, t % 3
            dgram[t] = quarters(product(eleft, i * DELAY, eright, j * DELAY, DELAY))
            dcross[t] = quarters(product(eleft, i * DELAY, eafter, j * DELAY, DELAY))
            return carry
        lax.fori_loop(0, 9, excess, 0)

        sub = lax.broadcasted_iota(jnp.int32, (8, UNIT), 0)

        def pick(block, start, row):
            rows = jnp.where(sub == row, own[block, pl.ds(pl.multiple_of(start, 8), 8), :], 0.0)
            line = jnp.sum(rows, axis=0, keepdims=True)
            return jnp.where(sub == 0, jnp.broadcast_to(line, (8, UNIT)), 0.0)
        ends = jnp.concatenate([pick(k, last * (DELAY - 8), last * 7) for k in range(LAGS)], 1)
        lead = jnp.concatenate([pick(l + 1, 0, 0) for l in range(LAGS)], 1)
        lead = lead * last.astype(jnp.float32)
        wgram[...] = (0.5 + last.astype(jnp.float32)) * contract(ends, ends, ((0,), (0,)), HIGH)
        wcross[...] = contract(ends, lead, ((0,), (0,)), HIGH)

    own_copy.wait()
    own_extra.wait()
    x_extra.wait_recv()

    @pl.when(gets_z)
    def _():
        z_extra.wait_recv()

    @pl.when((h == 1) & has_next)
    def _():
        d_extra.wait_recv()

    @pl.when((h == 0) & jnp.logical_not(has_next))
    def _():
        ext[pl.ds(9, 3), pl.ds(HALF, 8), :] = jnp.zeros((3, 8, UNIT), jnp.float32)

    @pl.when((h == 1) & jnp.logical_not(has_prev))
    def _():
        ext[pl.ds(0, 4), pl.ds(HALF, 8), :] = jnp.zeros((4, 8, UNIT), jnp.float32)

    @pl.when((h == 1) & jnp.logical_not(has_next))
    def _():
        ext[pl.ds(11, 1), pl.ds(HALF, 8), :] = jnp.zeros((1, 8, UNIT), jnp.float32)

    def chunk(step, carry):
        c = CHUNKS - 1 - step
        x_copy(c).wait_recv()

        @pl.when(gets_z)
        def _():
            z_copy(c).wait_recv()

        def unit(e, carry):
            prepare(ext[e + 1, pl.ds(pl.multiple_of(c * UNIT, UNIT), UNIT + 8), :],
                    pl.multiple_of(e * UNIT, UNIT), left, right, after)
            return carry
        lax.fori_loop(0, 11, unit, 0)

        def lag(p, carry):
            a = h * (3 - p) * UNIT
            b = a + p * UNIT
            acc[p] += product(left, a, right, b, 8 * UNIT)
            acc[LAGS + p] += product(left, a, after, b, 8 * UNIT)
            acc[2 * LAGS + p] += product(left, b, after, a, 8 * UNIT)
            return carry
        lax.fori_loop(0, LAGS, lag, 0)
        return carry
    lax.fori_loop(0, CHUNKS, chunk, 0)

    def term(n, k, l):
        if n < len(GRAM):
            return quarters(acc[l - k])
        return quarters(acc[LAGS + l - k] if l >= k else acc[2 * LAGS + k - l])

    blocks = GRAM + CROSS

    @pl.when(jnp.logical_not(edge))
    def _():
        for m in range(-LAGS + 1, LAGS):
            for first in (True, False):
                which = [n for n, (k, l) in enumerate(blocks) if l - k == m and (n < len(GRAM)) == first]
                if which:
                    value = term(which[0], *blocks[which[0]])
                    for n in which:
                        buf[pl.ds(n * UNIT, UNIT), :] = value

    @pl.when(edge)
    def _():
        last = jnp.where(at > 0, 1, 0).astype(jnp.float32)
        for n, (k, l) in enumerate(blocks):
            m = l - k
            value = term(n, k, l)
            less, ends = (dgram, wgram) if n < len(GRAM) else (dcross, wcross)
            for i in range(max(0, -m), min(2, 2 - m) + 1):
                value = value - less[3 * i + i + m] * ((1.0 - last) if i < k else last)
            value = value - ends[pl.ds(k * UNIT, UNIT), pl.ds(l * UNIT, UNIT)]
            buf[pl.ds(n * UNIT, UNIT), :] = value

    total = 2 * plane * pairs * piece
    if total > NB * UNIT:
        buf[pl.ds(NB * UNIT, total - NB * UNIT), :] = jnp.zeros((total - NB * UNIT, UNIT), jnp.float32)

    def rows(n, size, base=0):
        return pl.ds(pl.multiple_of(base + n * size, 8), size)

    part = plane * pairs * piece
    copy = remote(buf.at[rows(1 - core, part)], slot_a, as_.at[0], ar.at[0], core_peer)
    copy.start()
    copy.wait()
    base_a = core * part
    buf[rows(core, part), :] += slot_a[...]
    sub_part = pairs * piece
    copies = []
    for d in range(1, plane):
        there = (place + d) % plane
        copies.append(remote(buf.at[rows(there, sub_part, base_a)], slot_b.at[d - 1],
                             bs.at[d - 1], br.at[d - 1], plane_peer(d)))
        copies[-1].start()
    for c in copies:
        c.wait()
    base_b = base_a + place * sub_part
    value = buf[rows(0, sub_part, base_b), :]
    for d in range(1, plane):
        value = value + slot_b[d - 1]
    buf[rows(0, sub_part, base_b), :] = value
    copies = []
    for d in range(1, pairs):
        there = (q + d) % pairs
        copies.append(remote(buf.at[rows(there, piece, base_b)], slot_c.at[d - 1],
                             cs.at[d - 1], cr.at[d - 1], line_peer(d)))
        copies[-1].start()
    for c in copies:
        c.wait()
    base_c = base_b + q * piece
    value = buf[rows(0, piece, base_c), :]
    for d in range(1, pairs):
        value = value + slot_c[d - 1]
    mine = out.at[rows(0, piece, base_c)]
    out[rows(0, piece, base_c), :] = value

    copies = []
    for d in range(1, pairs):
        copies.append(remote(mine, mine, gcs.at[d - 1], gcr.at[d - 1], line_peer(d)))
        copies[-1].start()
    for c in copies:
        c.wait()
    mine = out.at[rows(0, sub_part, base_b)]
    copies = []
    for d in range(1, plane):
        copies.append(remote(mine, mine, gbs.at[d - 1], gbr.at[d - 1], plane_peer(d)))
        copies[-1].start()
    for c in copies:
        c.wait()
    mine = out.at[rows(0, part, base_a)]
    copy = remote(mine, mine, gas.at[0], gar.at[0], core_peer)
    copy.start()
    copy.wait()

    x_extra.wait_send()
    for c in range(CHUNKS):
        x_copy(c).wait_send()

    @pl.when(sends_z)
    def _():
        z_extra.wait_send()
        for c in range(CHUNKS):
            z_copy(c).wait_send()

    @pl.when((h == 0) & has_prev)
    def _():
        d_extra.wait_send()


def on_device(record):
    count, comps = record.shape
    groups, spans = lax.axis_size("grp"), lax.axis_size("span")
    devices = groups * spans
    lead = (LAGS - 1) * DELAY + 1
    last_row = count * devices - lead
    pairs = spans // 2
    piece = -(-NB * UNIT // (devices * 8)) * 8
    total = piece * devices
    dma = pltpu.SemaphoreType.DMA
    f32, bf16 = jnp.float32, jnp.bfloat16
    vmem = pl.BlockSpec(memory_space=pltpu.VMEM)
    sums = pl.pallas_call(
        functools.partial(sums_kernel, groups, spans, piece),
        out_shape=jax.ShapeDtypeStruct((total, comps), f32),
        in_specs=[pl.BlockSpec(memory_space=pl.ANY)], out_specs=vmem,
        scratch_shapes=[
            pltpu.VMEM((12, HALF + 8, UNIT), f32),
            pltpu.VMEM((LAGS + 1, DELAY, UNIT), f32),
            pltpu.VMEM((2 * UNIT, 11 * UNIT), bf16),
            pltpu.VMEM((11 * UNIT, 2 * UNIT), bf16),
            pltpu.VMEM((11 * UNIT, 2 * UNIT), bf16),
            pltpu.VMEM((3 * LAGS, 2 * UNIT, 2 * UNIT), f32),
            pltpu.VMEM((2 * UNIT, 3 * DELAY), bf16),
            pltpu.VMEM((3 * DELAY, 2 * UNIT), bf16),
            pltpu.VMEM((3 * DELAY, 2 * UNIT), bf16),
            pltpu.VMEM((9, UNIT, UNIT), f32),
            pltpu.VMEM((9, UNIT, UNIT), f32),
            pltpu.VMEM((LAGS * UNIT, LAGS * UNIT), f32),
            pltpu.VMEM((LAGS * UNIT, LAGS * UNIT), f32),
            pltpu.VMEM((total, UNIT), f32),
            pltpu.VMEM((total // 2, UNIT), f32),
            pltpu.VMEM((groups - 1, pairs * piece, UNIT), f32),
            pltpu.VMEM((pairs - 1, piece, UNIT), f32),
            dma((3,)), dma((CHUNKS,)), dma((CHUNKS,)), dma((CHUNKS,)), dma((CHUNKS,)), dma((3,)), dma((3,)),
            dma((1,)), dma((1,)), dma((groups - 1,)), dma((groups - 1,)), dma((pairs - 1,)), dma((pairs - 1,)),
            dma((pairs - 1,)), dma((pairs - 1,)), dma((groups - 1,)), dma((groups - 1,)), dma((1,)), dma((1,)),
        ],
        compiler_params=pltpu.CompilerParams(
            collective_id=0, has_side_effects=True, vmem_limit_bytes=56 << 20),
    )(record.reshape(LAGS, DELAY, comps))
    size = LAGS * comps
    return pl.pallas_call(
        functools.partial(solve_kernel, comps, 1.0 / last_row),
        out_shape=(jax.ShapeDtypeStruct((size, size), f32),) * 2,
        in_specs=[vmem], out_specs=(vmem, vmem),
        scratch_shapes=[
            pltpu.VMEM((LAGS, comps, 2 * size), f32),
            pltpu.VMEM((LAGS, comps, comps), f32),
        ],
        compiler_params=pltpu.CompilerParams(vmem_limit_bytes=48 << 20),
    )(sums)


def solution(mesh):
    placed = (P(AXES, None),)
    return jax.shard_map(
        on_device, mesh=mesh, in_specs=placed, out_specs=(P(), P()), check_vma=False
    )
```

```python
import functools

import jax
import jax.numpy as jnp
from jax import lax
from jax.experimental import pallas as pl
from jax.experimental.pallas import tpu as pltpu
from jax.sharding import PartitionSpec as P

LAGS = 4
DELAY = 1024
AXES = ("grp", "span")
HIGH = lax.Precision.HIGHEST
MESH = pl.DeviceIdType.MESH
UNIT = 128
HALF = DELAY // 2
CHUNKS = HALF // UNIT
GRAM = [(k, l) for k in range(LAGS) for l in range(k, LAGS)]
CROSS = [(k, l) for k in range(LAGS) for l in range(LAGS)]
NB = len(GRAM) + len(CROSS)


def contract(left, right, dims, precision=None):
    return lax.dot_general(
        left, right, (dims, ((), ())), precision=precision,
        preferred_element_type=jnp.float32,
    )


def factor(block):
    n = block.shape[0]
    groups = n // 8
    lane = lax.broadcasted_iota(jnp.int32, (8, n), 1)
    sub = lax.broadcasted_iota(jnp.int32, (8, n), 0)
    a = [block[8 * g:8 * g + 8, :] for g in range(groups)]
    b = [jnp.where(lane == sub + 8 * g, 1.0, 0.0) for g in range(groups)]

    def column(x, k):
        return jnp.broadcast_to(x[:, k:k + 1], (8, n))

    def line(x, i):
        return jnp.broadcast_to(x[i:i + 1, :], (8, n))

    def stack(rows):
        value = rows[0]
        for i in range(1, 8):
            value = jnp.where(sub == i, rows[i], value)
        return value

    for g in range(groups):
        cols = [column(a[g], 8 * g + j) for j in range(8)]
        s = [[line(cols[j], i) for j in range(i + 1)] for i in range(8)]
        rows = [line(a[g], i) for i in range(8)]
        lines = [line(b[g], i) for i in range(8)]
        inverse = []
        for r in range(8):
            inverse.append(1.0 / s[r][r])
            factors = [s[i][r] * inverse[r] for i in range(r + 1, 8)]
            for i in range(r + 1, 8):
                for j in range(r + 1, i + 1):
                    s[i][j] = s[i][j] - factors[i - r - 1] * s[j][r]
            for i in range(r + 1, 8):
                s[i][r] = factors[i - r - 1]
                rows[i] = rows[i] - s[i][r] * rows[r]
                lines[i] = lines[i] - s[i][r] * lines[r]
        scale = lax.rsqrt(stack([s[r][r] for r in range(8)]))
        left, right = list(rows), list(lines)
        for r in reversed(range(8)):
            left[r] = rows[r] * inverse[r]
            right[r] = lines[r] * inverse[r]
            for i in range(r + 1, 8):
                left[r] = left[r] - s[i][r] * left[i]
                right[r] = right[r] - s[i][r] * right[i]
        for h in range(g + 1, groups):
            old = a[h]
            for j in range(8):
                c = column(old, 8 * g + j)
                a[h] = a[h] - c * left[j]
                b[h] = b[h] - c * right[j]
        a[g] = jnp.where(lane >= sub + 8 * g, stack(rows) * scale, 0.0)
        b[g] = stack(lines) * scale
    return jnp.concatenate(a, 0), jnp.concatenate(b, 0)


def solve_kernel(comps, scale, gram_ref, cross_ref, tri_ref, op_ref, work, inverses):
    size = LAGS * comps
    for i in range(LAGS):
        rows = pl.ds(i * comps, comps)
        for j in range(LAGS):
            if j >= i:
                at = GRAM.index((i, j)) * comps
                work[i, :, pl.ds(j * comps, comps)] = gram_ref[pl.ds(at, comps), :] * scale
            at = CROSS.index((i, j)) * comps
            work[i, :, pl.ds(size + j * comps, comps)] = cross_ref[pl.ds(at, comps), :] * scale
        if i:
            work[i, :, pl.ds(0, i * comps)] = jnp.zeros((comps, i * comps), jnp.float32)
            tri_ref[rows, pl.ds(0, i * comps)] = jnp.zeros((comps, i * comps), jnp.float32)

    def step(i, carry):
        at = pl.multiple_of(i * comps, comps)
        upper, inverse = factor(work[i, :, pl.ds(at, comps)])
        inverses[i] = inverse
        work[i] = contract(inverse, work[i], ((1,), (0,)), HIGH)
        work[i, :, pl.ds(at, comps)] = upper

        def update(j, carry):
            to = pl.multiple_of(j * comps, comps)
            work[j] = work[j] - contract(work[i, :, pl.ds(to, comps)], work[i], ((0,), (0,)), HIGH)
            return carry
        lax.fori_loop(i + 1, LAGS, update, 0)
        return carry
    lax.fori_loop(0, LAGS, step, 0)

    for i in range(LAGS):
        for j in range(i, LAGS):
            tri_ref[pl.ds(i * comps, comps), pl.ds(j * comps, comps)] = work[i, :, pl.ds(j * comps, comps)]
    for b in range(LAGS):
        rest = jnp.concatenate(
            [work[i, :, pl.ds((LAGS + b) * comps, comps)] for i in range(LAGS)], 0)
        if b:
            rest = rest - contract(
                op_ref[:, pl.ds(0, b * comps)],
                tri_ref[pl.ds(0, b * comps), pl.ds(b * comps, comps)], ((1,), (0,)), HIGH)
        op_ref[:, pl.ds(b * comps, comps)] = contract(rest, inverses[b], ((1,), (1,)), HIGH)


def halves(x):
    spread = x * 65537.0
    high = spread - (spread - x)
    return high.astype(jnp.bfloat16), (x - high).astype(jnp.bfloat16)


def quarters(x):
    n = x.shape[0] // 2
    return (x[:n, :n] + x[:n, n:]) + (x[n:, :n] + x[n:, n:])


def prepare(window, at, left, right, after):
    cols = pl.ds(at, UNIT)
    rows = window[:UNIT]
    high, low = halves(rows)
    right[cols, pl.ds(0, UNIT)] = high
    right[cols, pl.ds(UNIT, UNIT)] = low
    high, low = halves(rows.T)
    left[pl.ds(0, UNIT), cols] = high
    left[pl.ds(UNIT, UNIT), cols] = low
    high, low = halves(pltpu.roll(window, window.shape[0] - 1, 0)[:UNIT])
    after[cols, pl.ds(0, UNIT)] = high
    after[cols, pl.ds(UNIT, UNIT)] = low


def product(left, lcol, right, rrow, depth):
    lcol = pl.multiple_of(lcol, UNIT)
    rrow = pl.multiple_of(rrow, UNIT)
    return jnp.dot(left[:, pl.ds(lcol, depth)], right[pl.ds(rrow, depth), :],
                   preferred_element_type=jnp.float32)


class Total:
    def __init__(self, remote, core, place, q, plane, pairs, piece, peers, refs):
        self.buf, self.out, self.slots = refs[0], refs[1], refs[2:5]
        self.sems = refs[5:]
        self.remote, self.piece = remote, piece
        self.sizes = (plane * pairs * piece, pairs * piece, piece)
        self.index, self.counts, self.peers = (core, place, q), (2, plane, pairs), peers
        self.base = [0]
        for size, index in zip(self.sizes, self.index):
            self.base.append(self.base[-1] + index * size)
        self.copies = []

    def rows(self, level, n):
        size = self.sizes[level]
        return pl.ds(pl.multiple_of(self.base[level] + n * size, 8), size)

    def send(self, level):
        self.copies = []
        for d in range(1, self.counts[level]):
            there = (self.index[level] + d) % self.counts[level]
            self.copies.append(self.remote(
                self.buf.at[self.rows(level, there)], self.slots[level].at[d - 1],
                self.sems[0].at[level, d - 1], self.sems[1].at[level, d - 1], self.peers[level](d)))
            self.copies[-1].start()

    def add(self, level):
        for copy in self.copies:
            copy.wait()
        mine = self.rows(level, self.index[level])
        value = self.buf[mine, :]
        for d in range(1, self.counts[level]):
            value = value + self.slots[level][d - 1]
        if level == 2:
            self.out[mine, :] = value
        else:
            self.buf[mine, :] = value

    def share(self, level):
        mine = self.out.at[self.rows(level, self.index[level])]
        self.copies = []
        for d in range(1, self.counts[level]):
            self.copies.append(self.remote(
                mine, mine, self.sems[2].at[level, d - 1], self.sems[3].at[level, d - 1], self.peers[level](d)))
            self.copies[-1].start()

    def wait(self):
        for copy in self.copies:
            copy.wait()


def sums_kernel(groups, spans, pieces, rec, gram_out, cross_out, ext, own, left, right, after, acc,
                eleft, eright, eafter, dgram, dcross, wgram, wcross,
                local_sem, xs, xr, zs, zr, es, er, *reduce_refs):
    grp, span = lax.axis_index("grp"), lax.axis_index("span")
    pairs = spans // 2
    h, q = span % 2, span // 2
    core, y = grp % 2, grp // 2
    plane, place = groups, y * 2 + h
    at, count = grp * pairs + q, groups * pairs
    has_prev, has_next = at > 0, at < count - 1

    def device(pair, side):
        pair = (pair + count) % count
        return (pair // pairs, (pair % pairs) * 2 + side)

    def plane_peer(d):
        there = (place + d) % plane
        return ((there // 2) * 2 + core, q * 2 + there % 2)

    def line_peer(d):
        return (grp, ((q + d) % pairs) * 2 + h)

    core_peer = (y * 2 + 1 - core, span)
    partner = (grp, q * 2 + 1 - h)
    z_to = device(at - 1 + 2 * h, h)
    sends_z = jnp.where(h == 0, at, count - 1 - at) > 0
    gets_z = jnp.where(h == 0, count - 1 - at, at) > 0

    own_copy = pltpu.make_async_copy(
        rec.at[:, pl.ds(h * HALF, HALF), :], ext.at[pl.ds(1 + 7 * h, 4), pl.ds(0, HALF), :], local_sem.at[0])
    own_extra = pltpu.make_async_copy(
        rec.at[:, pl.ds((1 - h) * HALF, 8), :], ext.at[pl.ds(1 + 6 * h, 4), pl.ds(HALF, 8), :], local_sem.at[1])
    own_copy.start()
    own_extra.start()
    edge = (at * 2 + h == 0) | (at * 2 + h == 2 * count - 1)
    full_copy = pltpu.make_async_copy(rec, own.at[pl.ds(0, LAGS)], local_sem.at[2])

    @pl.when(edge)
    def _():
        full_copy.start()

    barrier = pltpu.get_barrier_semaphore()

    def greet(to):
        pl.semaphore_signal(barrier, inc=1, device_id=to, device_id_type=MESH)

    greet(core_peer)
    for d in range(1, plane):
        greet(plane_peer(d))
    for d in range(1, pairs):
        greet(line_peer(d))

    @pl.when(has_prev)
    def _():
        greet(device(at - 1, h))

    @pl.when(has_next)
    def _():
        greet(device(at + 1, h))

    @pl.when((h == 0) & has_prev)
    def _():
        greet(device(at - 1, 1))

    @pl.when((h == 1) & has_next)
    def _():
        greet(device(at + 1, 0))

    pl.semaphore_wait(
        barrier, plane + pairs - 1
        + jnp.where(has_prev, 1, 0) + jnp.where(has_next, 1, 0)
        + jnp.where((h == 0) & has_prev, 1, 0) + jnp.where((h == 1) & has_next, 1, 0))

    def remote(src, dst, send, recv, to):
        return pltpu.make_async_remote_copy(
            src_ref=src, dst_ref=dst, send_sem=send, recv_sem=recv, device_id=to, device_id_type=MESH)

    def x_copy(c):
        return remote(
            rec.at[:, pl.ds((1 - h) * HALF + c * UNIT, UNIT), :],
            ext.at[pl.ds(4 + h, 4), pl.ds(c * UNIT, UNIT), :], xs.at[c], xr.at[c], partner)

    def z_copy(c):
        return remote(
            rec.at[pl.ds(h, 3), pl.ds(h * HALF + c * UNIT, UNIT), :],
            ext.at[pl.ds(9 - 8 * h, 3), pl.ds(c * UNIT, UNIT), :], zs.at[c], zr.at[c], z_to)

    x_extra = remote(
        rec.at[:, pl.ds(h * HALF, 8), :], ext.at[pl.ds(3 + 2 * h, 4), pl.ds(HALF, 8), :],
        es.at[0], er.at[0], partner)
    z_extra = remote(
        rec.at[pl.ds(h, 3), pl.ds((1 - h) * HALF, 8), :], ext.at[pl.ds(9 - 9 * h, 3), pl.ds(HALF, 8), :],
        es.at[1], er.at[1], z_to)
    d_extra = remote(
        rec.at[pl.ds(0, 1), pl.ds(0, 8), :], ext.at[pl.ds(11, 1), pl.ds(HALF, 8), :],
        es.at[2], er.at[2], device(at - 1, 1))

    x_extra.start()
    for c in reversed(range(CHUNKS)):
        x_copy(c).start()

    @pl.when(sends_z)
    def _():
        z_extra.start()
        for c in reversed(range(CHUNKS)):
            z_copy(c).start()

    @pl.when((h == 0) & has_prev)
    def _():
        d_extra.start()

    @pl.when(jnp.logical_not(gets_z))
    def _():
        ext[pl.ds(9 - 8 * h, 3), pl.ds(0, HALF), :] = jnp.zeros((3, HALF, UNIT), jnp.float32)

    acc[...] = jnp.zeros(acc.shape, jnp.float32)

    @pl.when(edge)
    def _():
        last = jnp.where(at > 0, 1, 0)
        own[LAGS, pl.ds(0, 8), :] = jnp.zeros((8, UNIT), jnp.float32)
        full_copy.wait()
        parts = DELAY // UNIT

        def unit(t, carry):
            block, row = t // parts, (t % parts) * UNIT
            rows = own[last + block, pl.ds(pl.multiple_of(row, UNIT), UNIT), :]
            more = t + 1
            tail = own[last + more // parts, pl.ds(pl.multiple_of((more % parts) * UNIT, UNIT), 8), :]
            prepare(jnp.concatenate([rows, tail], 0), pl.multiple_of(t * UNIT, UNIT), eleft, eright, eafter)
            return carry
        lax.fori_loop(0, 3 * parts, unit, 0)

        def excess(t, carry):
            i, j = t // 3, t % 3
            dgram[t] = quarters(product(eleft, i * DELAY, eright, j * DELAY, DELAY))
            dcross[t] = quarters(product(eleft, i * DELAY, eafter, j * DELAY, DELAY))
            return carry
        lax.fori_loop(0, 9, excess, 0)

        sub = lax.broadcasted_iota(jnp.int32, (8, UNIT), 0)

        def pick(block, start, row):
            rows = jnp.where(sub == row, own[block, pl.ds(pl.multiple_of(start, 8), 8), :], 0.0)
            line = jnp.sum(rows, axis=0, keepdims=True)
            return jnp.where(sub == 0, jnp.broadcast_to(line, (8, UNIT)), 0.0)
        ends = jnp.concatenate([pick(k, last * (DELAY - 8), last * 7) for k in range(LAGS)], 1)
        lead = jnp.concatenate([pick(l + 1, 0, 0) for l in range(LAGS)], 1)
        lead = lead * last.astype(jnp.float32)
        wgram[...] = (0.5 + last.astype(jnp.float32)) * contract(ends, ends, ((0,), (0,)), HIGH)
        wcross[...] = contract(ends, lead, ((0,), (0,)), HIGH)

    own_copy.wait()
    own_extra.wait()
    x_extra.wait_recv()

    @pl.when(gets_z)
    def _():
        z_extra.wait_recv()

    @pl.when((h == 1) & has_next)
    def _():
        d_extra.wait_recv()

    @pl.when((h == 0) & jnp.logical_not(has_next))
    def _():
        ext[pl.ds(9, 3), pl.ds(HALF, 8), :] = jnp.zeros((3, 8, UNIT), jnp.float32)

    @pl.when((h == 1) & jnp.logical_not(has_prev))
    def _():
        ext[pl.ds(0, 4), pl.ds(HALF, 8), :] = jnp.zeros((4, 8, UNIT), jnp.float32)

    @pl.when((h == 1) & jnp.logical_not(has_next))
    def _():
        ext[pl.ds(11, 1), pl.ds(HALF, 8), :] = jnp.zeros((1, 8, UNIT), jnp.float32)

    def chunk(step, carry):
        c = CHUNKS - 1 - step
        x_copy(c).wait_recv()

        @pl.when(gets_z)
        def _():
            z_copy(c).wait_recv()

        def unit(e, carry):
            prepare(ext[e + 1, pl.ds(pl.multiple_of(c * UNIT, UNIT), UNIT + 8), :],
                    pl.multiple_of(e * UNIT, UNIT), left, right, after)
            return carry
        lax.fori_loop(0, 11, unit, 0)

        def lag(p, carry):
            a = h * (3 - p) * UNIT
            b = a + p * UNIT
            acc[p] += product(left, a, right, b, 8 * UNIT)
            acc[LAGS + p] += product(left, a, after, b, 8 * UNIT)
            acc[2 * LAGS + p] += product(left, b, after, a, 8 * UNIT)
            return carry
        lax.fori_loop(0, LAGS, lag, 0)
        return carry
    lax.fori_loop(0, CHUNKS, chunk, 0)

    def term(n, k, l):
        if n < len(GRAM):
            return quarters(acc[l - k])
        return quarters(acc[LAGS + l - k] if l >= k else acc[2 * LAGS + k - l])

    blocks = GRAM + CROSS
    half = len(reduce_refs) // 2
    peers = (lambda d: core_peer, plane_peer, line_peer)
    gram, cross = (
        Total(remote, core, place, q, plane, pairs, piece, peers, (refs[0], out) + refs[1:])
        for piece, out, refs in zip(pieces, (gram_out, cross_out), (reduce_refs[:half], reduce_refs[half:])))

    def gather(total, numbers):
        @pl.when(jnp.logical_not(edge))
        def _():
            for m in range(-LAGS + 1, LAGS):
                which = [n for n in numbers if blocks[n][1] - blocks[n][0] == m]
                if which:
                    value = term(which[0], *blocks[which[0]])
                    for n in which:
                        total.buf[pl.ds((n - numbers[0]) * UNIT, UNIT), :] = value

        @pl.when(edge)
        def _():
            last = jnp.where(at > 0, 1, 0).astype(jnp.float32)
            for n in numbers:
                k, l = blocks[n]
                m = l - k
                value = term(n, k, l)
                less, ends = (dgram, wgram) if n < len(GRAM) else (dcross, wcross)
                for i in range(max(0, -m), min(2, 2 - m) + 1):
                    value = value - less[3 * i + i + m] * ((1.0 - last) if i < k else last)
                value = value - ends[pl.ds(k * UNIT, UNIT), pl.ds(l * UNIT, UNIT)]
                total.buf[pl.ds((n - numbers[0]) * UNIT, UNIT), :] = value
        used, size = len(numbers) * UNIT, total.buf.shape[0]
        if size > used:
            total.buf[pl.ds(used, size - used), :] = jnp.zeros((size - used, UNIT), jnp.float32)

    gather(gram, list(range(len(GRAM))))
    gram.send(0)
    gather(cross, list(range(len(GRAM), NB)))
    gram.add(0)
    gram.send(1)
    cross.send(0)
    cross.add(0)
    gram.add(1)
    gram.send(2)
    cross.send(1)
    gram.add(2)
    gram.share(2)
    cross.add(1)
    cross.send(2)
    gram.wait()
    gram.share(1)
    cross.add(2)
    cross.share(2)
    gram.wait()
    gram.share(0)
    cross.wait()
    cross.share(1)
    gram.wait()
    cross.wait()
    cross.share(0)
    cross.wait()

    x_extra.wait_send()
    for c in range(CHUNKS):
        x_copy(c).wait_send()

    @pl.when(sends_z)
    def _():
        z_extra.wait_send()
        for c in range(CHUNKS):
            z_copy(c).wait_send()

    @pl.when((h == 0) & has_prev)
    def _():
        d_extra.wait_send()


def on_device(record):
    count, comps = record.shape
    groups, spans = lax.axis_size("grp"), lax.axis_size("span")
    devices = groups * spans
    lead = (LAGS - 1) * DELAY + 1
    last_row = count * devices - lead
    pairs = spans // 2
    pieces = [-(-n * UNIT // (devices * 8)) * 8 for n in (len(GRAM), len(CROSS))]
    dma = pltpu.SemaphoreType.DMA
    f32, bf16 = jnp.float32, jnp.bfloat16
    vmem = pl.BlockSpec(memory_space=pltpu.VMEM)
    sums = pl.pallas_call(
        functools.partial(sums_kernel, groups, spans, pieces),
        out_shape=[jax.ShapeDtypeStruct((piece * devices, comps), f32) for piece in pieces],
        in_specs=[pl.BlockSpec(memory_space=pl.ANY)], out_specs=[vmem, vmem],
        scratch_shapes=[
            pltpu.VMEM((12, HALF + 8, UNIT), f32),
            pltpu.VMEM((LAGS + 1, DELAY, UNIT), f32),
            pltpu.VMEM((2 * UNIT, 11 * UNIT), bf16),
            pltpu.VMEM((11 * UNIT, 2 * UNIT), bf16),
            pltpu.VMEM((11 * UNIT, 2 * UNIT), bf16),
            pltpu.VMEM((3 * LAGS, 2 * UNIT, 2 * UNIT), f32),
            pltpu.VMEM((2 * UNIT, 3 * DELAY), bf16),
            pltpu.VMEM((3 * DELAY, 2 * UNIT), bf16),
            pltpu.VMEM((3 * DELAY, 2 * UNIT), bf16),
            pltpu.VMEM((9, UNIT, UNIT), f32),
            pltpu.VMEM((9, UNIT, UNIT), f32),
            pltpu.VMEM((LAGS * UNIT, LAGS * UNIT), f32),
            pltpu.VMEM((LAGS * UNIT, LAGS * UNIT), f32),
            dma((3,)), dma((CHUNKS,)), dma((CHUNKS,)), dma((CHUNKS,)), dma((CHUNKS,)), dma((3,)), dma((3,)),
            *(ref for piece in pieces for ref in (
                pltpu.VMEM((piece * devices, UNIT), f32),
                pltpu.VMEM((1, piece * devices // 2, UNIT), f32),
                pltpu.VMEM((groups - 1, pairs * piece, UNIT), f32),
                pltpu.VMEM((pairs - 1, piece, UNIT), f32),
                *(dma((3, max(groups, pairs) - 1)),) * 4)),
        ],
        compiler_params=pltpu.CompilerParams(
            collective_id=0, has_side_effects=True, vmem_limit_bytes=56 << 20),
    )(record.reshape(LAGS, DELAY, comps))
    size = LAGS * comps
    return pl.pallas_call(
        functools.partial(solve_kernel, comps, 1.0 / last_row),
        out_shape=(jax.ShapeDtypeStruct((size, size), f32),) * 2,
        in_specs=[vmem, vmem], out_specs=(vmem, vmem),
        scratch_shapes=[
            pltpu.VMEM((LAGS, comps, 2 * size), f32),
            pltpu.VMEM((LAGS, comps, comps), f32),
        ],
        compiler_params=pltpu.CompilerParams(vmem_limit_bytes=48 << 20),
    )(*sums)


def solution(mesh):
    placed = (P(AXES, None),)
    return jax.shard_map(
        on_device, mesh=mesh, in_specs=placed, out_specs=(P(), P()), check_vma=False
    )
```

```python
import functools

import jax
import jax.numpy as jnp
from jax import lax
from jax.experimental import pallas as pl
from jax.experimental.pallas import tpu as pltpu
from jax.sharding import PartitionSpec as P

LAGS = 4
DELAY = 1024
AXES = ("grp", "span")
HIGH = lax.Precision.HIGHEST
MESH = pl.DeviceIdType.MESH
UNIT = 128
HALF = DELAY // 2
CHUNKS = HALF // UNIT
GRAM = [(k, l) for k in range(LAGS) for l in range(k, LAGS)]
CROSS = [(k, l) for k in range(LAGS) for l in range(LAGS)]
NB = len(GRAM) + len(CROSS)


def contract(left, right, dims, precision=None):
    return lax.dot_general(
        left, right, (dims, ((), ())), precision=precision,
        preferred_element_type=jnp.float32,
    )


def factor(block):
    n = block.shape[0]
    groups = n // 8
    lane = lax.broadcasted_iota(jnp.int32, (8, n), 1)
    sub = lax.broadcasted_iota(jnp.int32, (8, n), 0)
    a = [block[8 * g:8 * g + 8, :] for g in range(groups)]
    b = [jnp.where(lane == sub + 8 * g, 1.0, 0.0) for g in range(groups)]

    def column(x, k):
        return jnp.broadcast_to(x[:, k:k + 1], (8, n))

    def line(x, i):
        return jnp.broadcast_to(x[i:i + 1, :], (8, n))

    def stack(rows):
        value = rows[0]
        for i in range(1, 8):
            value = jnp.where(sub == i, rows[i], value)
        return value

    for g in range(groups):
        cols = [column(a[g], 8 * g + j) for j in range(8)]
        s = [[line(cols[j], i) for j in range(i + 1)] for i in range(8)]
        rows = [line(a[g], i) for i in range(8)]
        lines = [line(b[g], i) for i in range(8)]
        inverse = []
        for r in range(8):
            inverse.append(1.0 / s[r][r])
            factors = [s[i][r] * inverse[r] for i in range(r + 1, 8)]
            for i in range(r + 1, 8):
                for j in range(r + 1, i + 1):
                    s[i][j] = s[i][j] - factors[i - r - 1] * s[j][r]
            for i in range(r + 1, 8):
                s[i][r] = factors[i - r - 1]
                rows[i] = rows[i] - s[i][r] * rows[r]
                lines[i] = lines[i] - s[i][r] * lines[r]
        scale = lax.rsqrt(stack([s[r][r] for r in range(8)]))
        left, right = list(rows), list(lines)
        for r in reversed(range(8)):
            left[r] = rows[r] * inverse[r]
            right[r] = lines[r] * inverse[r]
            for i in range(r + 1, 8):
                left[r] = left[r] - s[i][r] * left[i]
                right[r] = right[r] - s[i][r] * right[i]
        for h in range(g + 1, groups):
            old = a[h]
            for j in range(8):
                c = column(old, 8 * g + j)
                a[h] = a[h] - c * left[j]
                b[h] = b[h] - c * right[j]
        a[g] = jnp.where(lane >= sub + 8 * g, stack(rows) * scale, 0.0)
        b[g] = stack(lines) * scale
    return jnp.concatenate(a, 0), jnp.concatenate(b, 0)


class Solve:
    def __init__(self, scale, gram, cross, tri, op, work, mid, inverses):
        self.scale, self.gram, self.cross, self.tri, self.op = scale, gram, cross, tri, op
        self.work, self.mid, self.inverses = work, mid, inverses

    def load(self):
        for i in range(LAGS):
            for j in range(LAGS):
                to = pl.ds(j * UNIT, UNIT)
                if j >= i:
                    at = GRAM.index((i, j)) * UNIT
                    self.work[i, :, to] = self.gram[pl.ds(at, UNIT), :] * self.scale
                else:
                    self.work[i, :, to] = jnp.zeros((UNIT, UNIT), jnp.float32)

    def step(self, i):
        work = self.work
        at = pl.ds(pl.multiple_of(i * UNIT, UNIT), UNIT)
        upper, inverse = factor(work[i, :, at])
        self.inverses[i] = inverse
        work[i] = contract(inverse, work[i], ((1,), (0,)), HIGH)
        work[i, :, at] = upper

        def update(j, carry):
            to = pl.ds(pl.multiple_of(j * UNIT, UNIT), UNIT)
            work[j] = work[j] - contract(work[i, :, to], work[i], ((0,), (0,)), HIGH)
            return carry
        lax.fori_loop(i + 1, LAGS, update, 0)

    def finish(self):
        work, mid, tri, op = self.work, self.mid, self.tri, self.op
        for i in range(LAGS):
            rows = pl.ds(i * UNIT, UNIT)
            tri[rows, pl.ds(i * UNIT, (LAGS - i) * UNIT)] = work[i, :, pl.ds(i * UNIT, (LAGS - i) * UNIT)]
            if i:
                tri[rows, pl.ds(0, i * UNIT)] = jnp.zeros((UNIT, i * UNIT), jnp.float32)
            right = jnp.concatenate(
                [self.cross[pl.ds(CROSS.index((i, j)) * UNIT, UNIT), :] for j in range(LAGS)], 1) * self.scale
            if i:
                over = jnp.concatenate([work[j, :, rows] for j in range(i)], 0)
                right = right - contract(over, mid[pl.ds(0, i * UNIT), :], ((0,), (0,)), HIGH)
            mid[rows, :] = contract(self.inverses[i], right, ((1,), (0,)), HIGH)
        for b in range(LAGS):
            cols = pl.ds(b * UNIT, UNIT)
            rest = mid[:, cols]
            if b:
                rest = rest - contract(
                    op[:, pl.ds(0, b * UNIT)], tri[pl.ds(0, b * UNIT), cols], ((1,), (0,)), HIGH)
            op[:, cols] = contract(rest, self.inverses[b], ((1,), (1,)), HIGH)


def halves(x):
    spread = x * 65537.0
    high = spread - (spread - x)
    return high.astype(jnp.bfloat16), (x - high).astype(jnp.bfloat16)


def quarters(x):
    n = x.shape[0] // 2
    return (x[:n, :n] + x[:n, n:]) + (x[n:, :n] + x[n:, n:])


def prepare(window, at, left, right, after):
    cols = pl.ds(at, UNIT)
    rows = window[:UNIT]
    high, low = halves(rows)
    right[cols, pl.ds(0, UNIT)] = high
    right[cols, pl.ds(UNIT, UNIT)] = low
    high, low = halves(rows.T)
    left[pl.ds(0, UNIT), cols] = high
    left[pl.ds(UNIT, UNIT), cols] = low
    high, low = halves(pltpu.roll(window, window.shape[0] - 1, 0)[:UNIT])
    after[cols, pl.ds(0, UNIT)] = high
    after[cols, pl.ds(UNIT, UNIT)] = low


def product(left, lcol, right, rrow, depth):
    lcol = pl.multiple_of(lcol, UNIT)
    rrow = pl.multiple_of(rrow, UNIT)
    return jnp.dot(left[:, pl.ds(lcol, depth)], right[pl.ds(rrow, depth), :],
                   preferred_element_type=jnp.float32)


class Total:
    def __init__(self, remote, core, place, q, plane, pairs, piece, peers, refs):
        self.buf, self.out, self.slots = refs[0], refs[1], refs[2:5]
        self.sems = refs[5:]
        self.remote, self.piece = remote, piece
        self.sizes = (plane * pairs * piece, pairs * piece, piece)
        self.index, self.counts, self.peers = (core, place, q), (2, plane, pairs), peers
        self.base = [0]
        for size, index in zip(self.sizes, self.index):
            self.base.append(self.base[-1] + index * size)
        self.copies = []

    def rows(self, level, n):
        size = self.sizes[level]
        return pl.ds(pl.multiple_of(self.base[level] + n * size, 8), size)

    def send(self, level):
        self.copies = []
        for d in range(1, self.counts[level]):
            there = (self.index[level] + d) % self.counts[level]
            self.copies.append(self.remote(
                self.buf.at[self.rows(level, there)], self.slots[level].at[d - 1],
                self.sems[0].at[level, d - 1], self.sems[1].at[level, d - 1], self.peers[level](d)))
            self.copies[-1].start()

    def add(self, level):
        for copy in self.copies:
            copy.wait()
        mine = self.rows(level, self.index[level])
        value = self.buf[mine, :]
        for d in range(1, self.counts[level]):
            value = value + self.slots[level][d - 1]
        if level == 2:
            self.out[mine, :] = value
        else:
            self.buf[mine, :] = value

    def share(self, level, start=True):
        mine = self.out.at[self.rows(level, self.index[level])]
        self.copies = []
        for d in range(1, self.counts[level]):
            self.copies.append(self.remote(
                mine, mine, self.sems[2].at[level, d - 1], self.sems[3].at[level, d - 1], self.peers[level](d)))
        if start:
            self.start()

    def start(self):
        for copy in self.copies:
            copy.start()

    def wait(self):
        for copy in self.copies:
            copy.wait()


def whole_kernel(groups, spans, pieces, scale, rec, tri, op, gram_out, cross_out, work, mid, inverses, ext, own, left, right, after, acc,
                eleft, eright, eafter, dgram, dcross, wgram, wcross,
                local_sem, xs, xr, zs, zr, es, er, *reduce_refs):
    grp, span = lax.axis_index("grp"), lax.axis_index("span")
    pairs = spans // 2
    h, q = span % 2, span // 2
    core, y = grp % 2, grp // 2
    plane, place = groups, y * 2 + h
    at, count = grp * pairs + q, groups * pairs
    has_prev, has_next = at > 0, at < count - 1

    def device(pair, side):
        pair = (pair + count) % count
        return (pair // pairs, (pair % pairs) * 2 + side)

    def plane_peer(d):
        there = (place + d) % plane
        return ((there // 2) * 2 + core, q * 2 + there % 2)

    def line_peer(d):
        return (grp, ((q + d) % pairs) * 2 + h)

    core_peer = (y * 2 + 1 - core, span)
    partner = (grp, q * 2 + 1 - h)
    z_to = device(at - 1 + 2 * h, h)
    sends_z = jnp.where(h == 0, at, count - 1 - at) > 0
    gets_z = jnp.where(h == 0, count - 1 - at, at) > 0

    own_copy = pltpu.make_async_copy(
        rec.at[:, pl.ds(h * HALF, HALF), :], ext.at[pl.ds(1 + 7 * h, 4), pl.ds(0, HALF), :], local_sem.at[0])
    own_extra = pltpu.make_async_copy(
        rec.at[:, pl.ds((1 - h) * HALF, 8), :], ext.at[pl.ds(1 + 6 * h, 4), pl.ds(HALF, 8), :], local_sem.at[1])
    own_copy.start()
    own_extra.start()
    edge = (at * 2 + h == 0) | (at * 2 + h == 2 * count - 1)
    full_copy = pltpu.make_async_copy(rec, own.at[pl.ds(0, LAGS)], local_sem.at[2])

    @pl.when(edge)
    def _():
        full_copy.start()

    barrier = pltpu.get_barrier_semaphore()

    def greet(to):
        pl.semaphore_signal(barrier, inc=1, device_id=to, device_id_type=MESH)

    greet(core_peer)
    for d in range(1, plane):
        greet(plane_peer(d))
    for d in range(1, pairs):
        greet(line_peer(d))

    @pl.when(has_prev)
    def _():
        greet(device(at - 1, h))

    @pl.when(has_next)
    def _():
        greet(device(at + 1, h))

    @pl.when((h == 0) & has_prev)
    def _():
        greet(device(at - 1, 1))

    @pl.when((h == 1) & has_next)
    def _():
        greet(device(at + 1, 0))

    pl.semaphore_wait(
        barrier, plane + pairs - 1
        + jnp.where(has_prev, 1, 0) + jnp.where(has_next, 1, 0)
        + jnp.where((h == 0) & has_prev, 1, 0) + jnp.where((h == 1) & has_next, 1, 0))

    def remote(src, dst, send, recv, to):
        return pltpu.make_async_remote_copy(
            src_ref=src, dst_ref=dst, send_sem=send, recv_sem=recv, device_id=to, device_id_type=MESH)

    def x_copy(c):
        return remote(
            rec.at[:, pl.ds((1 - h) * HALF + c * UNIT, UNIT), :],
            ext.at[pl.ds(4 + h, 4), pl.ds(c * UNIT, UNIT), :], xs.at[c], xr.at[c], partner)

    def z_copy(c):
        return remote(
            rec.at[pl.ds(h, 3), pl.ds(h * HALF + c * UNIT, UNIT), :],
            ext.at[pl.ds(9 - 8 * h, 3), pl.ds(c * UNIT, UNIT), :], zs.at[c], zr.at[c], z_to)

    x_extra = remote(
        rec.at[:, pl.ds(h * HALF, 8), :], ext.at[pl.ds(3 + 2 * h, 4), pl.ds(HALF, 8), :],
        es.at[0], er.at[0], partner)
    z_extra = remote(
        rec.at[pl.ds(h, 3), pl.ds((1 - h) * HALF, 8), :], ext.at[pl.ds(9 - 9 * h, 3), pl.ds(HALF, 8), :],
        es.at[1], er.at[1], z_to)
    d_extra = remote(
        rec.at[pl.ds(0, 1), pl.ds(0, 8), :], ext.at[pl.ds(11, 1), pl.ds(HALF, 8), :],
        es.at[2], er.at[2], device(at - 1, 1))

    x_extra.start()
    for c in reversed(range(CHUNKS)):
        x_copy(c).start()

    @pl.when(sends_z)
    def _():
        z_extra.start()
        for c in reversed(range(CHUNKS)):
            z_copy(c).start()

    @pl.when((h == 0) & has_prev)
    def _():
        d_extra.start()

    @pl.when(jnp.logical_not(gets_z))
    def _():
        ext[pl.ds(9 - 8 * h, 3), pl.ds(0, HALF), :] = jnp.zeros((3, HALF, UNIT), jnp.float32)

    acc[...] = jnp.zeros(acc.shape, jnp.float32)

    @pl.when(edge)
    def _():
        last = jnp.where(at > 0, 1, 0)
        own[LAGS, pl.ds(0, 8), :] = jnp.zeros((8, UNIT), jnp.float32)
        full_copy.wait()
        parts = DELAY // UNIT

        def unit(t, carry):
            block, row = t // parts, (t % parts) * UNIT
            rows = own[last + block, pl.ds(pl.multiple_of(row, UNIT), UNIT), :]
            more = t + 1
            tail = own[last + more // parts, pl.ds(pl.multiple_of((more % parts) * UNIT, UNIT), 8), :]
            prepare(jnp.concatenate([rows, tail], 0), pl.multiple_of(t * UNIT, UNIT), eleft, eright, eafter)
            return carry
        lax.fori_loop(0, 3 * parts, unit, 0)

        def excess(t, carry):
            i, j = t // 3, t % 3
            dgram[t] = quarters(product(eleft, i * DELAY, eright, j * DELAY, DELAY))
            dcross[t] = quarters(product(eleft, i * DELAY, eafter, j * DELAY, DELAY))
            return carry
        lax.fori_loop(0, 9, excess, 0)

        sub = lax.broadcasted_iota(jnp.int32, (8, UNIT), 0)

        def pick(block, start, row):
            rows = jnp.where(sub == row, own[block, pl.ds(pl.multiple_of(start, 8), 8), :], 0.0)
            line = jnp.sum(rows, axis=0, keepdims=True)
            return jnp.where(sub == 0, jnp.broadcast_to(line, (8, UNIT)), 0.0)
        ends = jnp.concatenate([pick(k, last * (DELAY - 8), last * 7) for k in range(LAGS)], 1)
        lead = jnp.concatenate([pick(l + 1, 0, 0) for l in range(LAGS)], 1)
        lead = lead * last.astype(jnp.float32)
        wgram[...] = (0.5 + last.astype(jnp.float32)) * contract(ends, ends, ((0,), (0,)), HIGH)
        wcross[...] = contract(ends, lead, ((0,), (0,)), HIGH)

    own_copy.wait()
    own_extra.wait()
    x_extra.wait_recv()

    @pl.when(gets_z)
    def _():
        z_extra.wait_recv()

    @pl.when((h == 1) & has_next)
    def _():
        d_extra.wait_recv()

    @pl.when((h == 0) & jnp.logical_not(has_next))
    def _():
        ext[pl.ds(9, 3), pl.ds(HALF, 8), :] = jnp.zeros((3, 8, UNIT), jnp.float32)

    @pl.when((h == 1) & jnp.logical_not(has_prev))
    def _():
        ext[pl.ds(0, 4), pl.ds(HALF, 8), :] = jnp.zeros((4, 8, UNIT), jnp.float32)

    @pl.when((h == 1) & jnp.logical_not(has_next))
    def _():
        ext[pl.ds(11, 1), pl.ds(HALF, 8), :] = jnp.zeros((1, 8, UNIT), jnp.float32)

    def load(c):
        def unit(t, base):
            e = base + t
            prepare(ext[e + 1, pl.ds(pl.multiple_of(c * UNIT, UNIT), UNIT + 8), :],
                    pl.multiple_of(e * UNIT, UNIT), left, right, after)
            return base
        lax.fori_loop(0, 4, unit, 7 * h)
        x_copy(c).wait_recv()

        @pl.when(gets_z)
        def _():
            z_copy(c).wait_recv()
        lax.fori_loop(0, 7, unit, 4 * (1 - h))

    def gram_lags():
        def lag(p, carry):
            a = h * (3 - p) * UNIT
            acc[p] += product(left, a, right, a + p * UNIT, 8 * UNIT)
            return carry
        lax.fori_loop(0, LAGS, lag, 0)

    def cross_lags():
        def lag(p, carry):
            a = h * (3 - p) * UNIT
            b = a + p * UNIT
            acc[LAGS + p] += product(left, a, after, b, 8 * UNIT)
            acc[2 * LAGS + p] += product(left, b, after, a, 8 * UNIT)
            return carry
        lax.fori_loop(0, LAGS, lag, 0)

    def chunk(step, carry):
        load(CHUNKS - 1 - step)
        gram_lags()
        cross_lags()
        return carry
    lax.fori_loop(0, CHUNKS - 1, chunk, 0)
    load(0)
    gram_lags()

    def term(n, k, l):
        if n < len(GRAM):
            return quarters(acc[l - k])
        return quarters(acc[LAGS + l - k] if l >= k else acc[2 * LAGS + k - l])

    blocks = GRAM + CROSS
    half = len(reduce_refs) // 2
    peers = (lambda d: core_peer, plane_peer, line_peer)
    gram, cross = (
        Total(remote, core, place, q, plane, pairs, piece, peers, (refs[0], out) + refs[1:])
        for piece, out, refs in zip(pieces, (gram_out, cross_out), (reduce_refs[:half], reduce_refs[half:])))

    def gather(total, numbers):
        @pl.when(jnp.logical_not(edge))
        def _():
            for m in range(-LAGS + 1, LAGS):
                which = [n for n in numbers if blocks[n][1] - blocks[n][0] == m]
                if which:
                    value = term(which[0], *blocks[which[0]])
                    for n in which:
                        total.buf[pl.ds((n - numbers[0]) * UNIT, UNIT), :] = value

        @pl.when(edge)
        def _():
            last = jnp.where(at > 0, 1, 0).astype(jnp.float32)
            for n in numbers:
                k, l = blocks[n]
                m = l - k
                value = term(n, k, l)
                less, ends = (dgram, wgram) if n < len(GRAM) else (dcross, wcross)
                for i in range(max(0, -m), min(2, 2 - m) + 1):
                    value = value - less[3 * i + i + m] * ((1.0 - last) if i < k else last)
                value = value - ends[pl.ds(k * UNIT, UNIT), pl.ds(l * UNIT, UNIT)]
                total.buf[pl.ds((n - numbers[0]) * UNIT, UNIT), :] = value
        used, size = len(numbers) * UNIT, total.buf.shape[0]
        if size > used:
            total.buf[pl.ds(used, size - used), :] = jnp.zeros((size - used, UNIT), jnp.float32)

    gather(gram, list(range(len(GRAM))))
    gram.send(0)
    cross_lags()
    gather(cross, list(range(len(GRAM), NB)))
    gram.add(0)
    gram.send(1)
    cross.send(0)
    cross.add(0)
    gram.add(1)
    gram.send(2)
    cross.send(1)
    gram.add(2)
    gram.share(2)
    cross.add(1)
    cross.send(2)
    gram.wait()
    gram.share(1)
    cross.add(2)
    cross.share(2)
    gram.wait()
    gram.share(0)
    cross.wait()
    cross.share(1)
    gram.wait()

    solve = Solve(scale, gram_out, cross_out, tri, op, work, mid, inverses)
    solve.load()

    shared = list(cross.copies)
    cross.share(0, start=False)

    def step(i, carry):
        solve.step(i)

        @pl.when(i == 0)
        def _():
            for copy in shared:
                copy.wait()
            cross.start()
        return carry
    lax.fori_loop(0, LAGS, step, 0)
    cross.wait()
    solve.finish()

    x_extra.wait_send()
    for c in range(CHUNKS):
        x_copy(c).wait_send()

    @pl.when(sends_z)
    def _():
        z_extra.wait_send()
        for c in range(CHUNKS):
            z_copy(c).wait_send()

    @pl.when((h == 0) & has_prev)
    def _():
        d_extra.wait_send()


def on_device(record):
    count, comps = record.shape
    groups, spans = lax.axis_size("grp"), lax.axis_size("span")
    devices = groups * spans
    lead = (LAGS - 1) * DELAY + 1
    last_row = count * devices - lead
    pairs = spans // 2
    pieces = [-(-n * UNIT // (devices * 8)) * 8 for n in (len(GRAM), len(CROSS))]
    dma = pltpu.SemaphoreType.DMA
    f32, bf16 = jnp.float32, jnp.bfloat16
    vmem = pl.BlockSpec(memory_space=pltpu.VMEM)
    size = LAGS * comps
    return pl.pallas_call(
        functools.partial(whole_kernel, groups, spans, pieces, 1.0 / last_row),
        out_shape=(jax.ShapeDtypeStruct((size, size), f32),) * 2,
        in_specs=[pl.BlockSpec(memory_space=pl.ANY)], out_specs=(vmem, vmem),
        scratch_shapes=[
            *(pltpu.VMEM((piece * devices, UNIT), f32) for piece in pieces),
            pltpu.VMEM((LAGS, UNIT, size), f32),
            pltpu.VMEM((size, size), f32),
            pltpu.VMEM((LAGS, UNIT, UNIT), f32),
            pltpu.VMEM((12, HALF + 8, UNIT), f32),
            pltpu.VMEM((LAGS + 1, DELAY, UNIT), f32),
            pltpu.VMEM((2 * UNIT, 11 * UNIT), bf16),
            pltpu.VMEM((11 * UNIT, 2 * UNIT), bf16),
            pltpu.VMEM((11 * UNIT, 2 * UNIT), bf16),
            pltpu.VMEM((3 * LAGS, 2 * UNIT, 2 * UNIT), f32),
            pltpu.VMEM((2 * UNIT, 3 * DELAY), bf16),
            pltpu.VMEM((3 * DELAY, 2 * UNIT), bf16),
            pltpu.VMEM((3 * DELAY, 2 * UNIT), bf16),
            pltpu.VMEM((9, UNIT, UNIT), f32),
            pltpu.VMEM((9, UNIT, UNIT), f32),
            pltpu.VMEM((LAGS * UNIT, LAGS * UNIT), f32),
            pltpu.VMEM((LAGS * UNIT, LAGS * UNIT), f32),
            dma((3,)), dma((CHUNKS,)), dma((CHUNKS,)), dma((CHUNKS,)), dma((CHUNKS,)), dma((3,)), dma((3,)),
            *(ref for piece in pieces for ref in (
                pltpu.VMEM((piece * devices, UNIT), f32),
                pltpu.VMEM((1, piece * devices // 2, UNIT), f32),
                pltpu.VMEM((groups - 1, pairs * piece, UNIT), f32),
                pltpu.VMEM((pairs - 1, piece, UNIT), f32),
                *(dma((3, max(groups, pairs) - 1)),) * 4)),
        ],
        compiler_params=pltpu.CompilerParams(
            collective_id=0, has_side_effects=True, vmem_limit_bytes=56 << 20),
    )(record.reshape(LAGS, DELAY, comps))


def solution(mesh):
    placed = (P(AXES, None),)
    return jax.shard_map(
        on_device, mesh=mesh, in_specs=placed, out_specs=(P(), P()), check_vma=False
    )
```

```python
import functools

import jax
import jax.numpy as jnp
from jax import lax
from jax.experimental import pallas as pl
from jax.experimental.pallas import tpu as pltpu
from jax.sharding import PartitionSpec as P

LAGS = 4
DELAY = 1024
AXES = ("grp", "span")
HIGH = lax.Precision.HIGHEST
MESH = pl.DeviceIdType.MESH
UNIT = 128
HALF = DELAY // 2
CHUNKS = HALF // UNIT
GRAM = [(k, l) for k in range(LAGS) for l in range(k, LAGS)]
CROSS = [(k, l) for k in range(LAGS) for l in range(LAGS)]
NB = len(GRAM) + len(CROSS)


def contract(left, right, dims, precision=None):
    return lax.dot_general(
        left, right, (dims, ((), ())), precision=precision,
        preferred_element_type=jnp.float32,
    )


def factor(block):
    n = block.shape[0]
    groups = n // 8
    lane = lax.broadcasted_iota(jnp.int32, (8, n), 1)
    sub = lax.broadcasted_iota(jnp.int32, (8, n), 0)
    a = [block[8 * g:8 * g + 8, :] for g in range(groups)]
    b = [jnp.where(lane == sub + 8 * g, 1.0, 0.0) for g in range(groups)]

    def column(x, k):
        return jnp.broadcast_to(x[:, k:k + 1], (8, n))

    def line(x, i):
        return jnp.broadcast_to(x[i:i + 1, :], (8, n))

    def stack(rows):
        value = rows[0]
        for i in range(1, 8):
            value = jnp.where(sub == i, rows[i], value)
        return value

    for g in range(groups):
        cols = [column(a[g], 8 * g + j) for j in range(8)]
        s = [[line(cols[j], i) for j in range(i + 1)] for i in range(8)]
        rows = [line(a[g], i) for i in range(8)]
        lines = [line(b[g], i) for i in range(8)]
        inverse = []
        for r in range(8):
            inverse.append(1.0 / s[r][r])
            factors = [s[i][r] * inverse[r] for i in range(r + 1, 8)]
            for i in range(r + 1, 8):
                for j in range(r + 1, i + 1):
                    s[i][j] = s[i][j] - factors[i - r - 1] * s[j][r]
            for i in range(r + 1, 8):
                s[i][r] = factors[i - r - 1]
                rows[i] = rows[i] - s[i][r] * rows[r]
                lines[i] = lines[i] - s[i][r] * lines[r]
        scale = lax.rsqrt(stack([s[r][r] for r in range(8)]))
        left, right = list(rows), list(lines)
        for r in reversed(range(8)):
            left[r] = rows[r] * inverse[r]
            right[r] = lines[r] * inverse[r]
            for i in range(r + 1, 8):
                left[r] = left[r] - s[i][r] * left[i]
                right[r] = right[r] - s[i][r] * right[i]
        for h in range(g + 1, groups):
            old = a[h]
            for j in range(8):
                c = column(old, 8 * g + j)
                a[h] = a[h] - c * left[j]
                b[h] = b[h] - c * right[j]
        a[g] = jnp.where(lane >= sub + 8 * g, stack(rows) * scale, 0.0)
        b[g] = stack(lines) * scale
    return jnp.concatenate(a, 0), jnp.concatenate(b, 0)


class Solve:
    def __init__(self, scale, gram, cross, tri, op, work, mid, inverse):
        self.scale, self.gram, self.cross, self.tri, self.op = scale, gram, cross, tri, op
        self.work, self.mid, self.inverse = work, mid, inverse

    def load(self):
        for n, (i, j) in enumerate(GRAM):
            self.work[cut(i), cut(j)] = self.gram[cut(n), :] * self.scale
        self.inverse[...] = jnp.zeros(self.inverse.shape, jnp.float32)

    def load_cross(self):
        for n, (i, j) in enumerate(CROSS):
            self.mid[cut(i), cut(j)] = self.cross[cut(n), :] * self.scale

    def step(self, k):
        work, rest = self.work, LAGS - k - 1
        upper, inverse = factor(work[cut(k), cut(k)])
        work[cut(k), cut(k)] = upper
        self.inverse[cut(k), cut(k)] = inverse
        if rest:
            work[cut(k), cut(k + 1, rest)] = contract(
                inverse, work[cut(k), cut(k + 1, rest)], ((1,), (0,)), HIGH)
        for j in range(k + 1, LAGS):
            to = (cut(j), cut(j, LAGS - j))
            work[to] = work[to] - contract(work[cut(k), cut(j)], work[cut(k), to[1]], ((0,), (0,)), HIGH)

    def invert(self, k):
        inverse = self.inverse
        if k:
            inverse[cut(k), cut(0, k)] = contract(
                inverse[cut(k), cut(k)], inverse[cut(k), cut(0, k)], ((1,), (0,)), HIGH)
        if k < LAGS - 1:
            to = (cut(k + 1, LAGS - k - 1), cut(0, k + 1))
            inverse[to] = inverse[to] - contract(
                self.work[cut(k), to[0]], inverse[cut(k), to[1]], ((0,), (0,)), HIGH)

    def apply(self, k):
        mid = self.mid
        mid[cut(k), :] = contract(self.inverse[cut(k), cut(k)], mid[cut(k), :], ((1,), (0,)), HIGH)
        if k < LAGS - 1:
            below = cut(k + 1, LAGS - k - 1)
            mid[below, :] = mid[below, :] - contract(
                self.work[cut(k), below], mid[cut(k), :], ((0,), (0,)), HIGH)

    def operate(self, rows, cols, depth):
        self.op[rows, cols] = contract(
            self.mid[rows, cut(0, depth)], self.inverse[cols, cut(0, depth)], ((1,), (1,)), HIGH)

    def triangle(self):
        for i in range(LAGS):
            self.tri[cut(i), cut(i, LAGS - i)] = self.work[cut(i), cut(i, LAGS - i)]
            if i:
                self.tri[cut(i), cut(0, i)] = jnp.zeros((UNIT, i * UNIT), jnp.float32)

    def second_half(self):
        self.load_cross()
        self.step(2)
        self.apply(0)
        self.apply(1)
        self.step(3)
        self.apply(2)
        self.invert(2)
        self.operate(cut(0, 3), cut(0, 3), 3)
        self.apply(3)
        self.invert(3)
        self.operate(cut(0, 3), cut(3), 4)
        self.operate(cut(3), cut(0, 4), 4)
        self.triangle()


def cut(n, count=1):
    return pl.ds(n * UNIT, count * UNIT)


def halves(x):
    spread = x * 65537.0
    high = spread - (spread - x)
    return high.astype(jnp.bfloat16), (x - high).astype(jnp.bfloat16)


def quarters(x):
    n = x.shape[0] // 2
    return (x[:n, :n] + x[:n, n:]) + (x[n:, :n] + x[n:, n:])


def prepare(window, at, left, right, after):
    cols = pl.ds(at, UNIT)
    rows = window[:UNIT]
    high, low = halves(rows)
    right[cols, pl.ds(0, UNIT)] = high
    right[cols, pl.ds(UNIT, UNIT)] = low
    high, low = halves(rows.T)
    left[pl.ds(0, UNIT), cols] = high
    left[pl.ds(UNIT, UNIT), cols] = low
    high, low = halves(pltpu.roll(window, window.shape[0] - 1, 0)[:UNIT])
    after[cols, pl.ds(0, UNIT)] = high
    after[cols, pl.ds(UNIT, UNIT)] = low


def product(left, lcol, right, rrow, depth):
    lcol = pl.multiple_of(lcol, UNIT)
    rrow = pl.multiple_of(rrow, UNIT)
    return jnp.dot(left[:, pl.ds(lcol, depth)], right[pl.ds(rrow, depth), :],
                   preferred_element_type=jnp.float32)


class Total:
    def __init__(self, remote, core, place, q, plane, pairs, piece, peers, refs):
        self.buf, self.out, self.slots = refs[0], refs[1], refs[2:5]
        self.sems = refs[5:]
        self.remote, self.piece = remote, piece
        self.sizes = (plane * pairs * piece, pairs * piece, piece)
        self.index, self.counts, self.peers = (core, place, q), (2, plane, pairs), peers
        self.base = [0]
        for size, index in zip(self.sizes, self.index):
            self.base.append(self.base[-1] + index * size)
        self.copies = []

    def rows(self, level, n):
        size = self.sizes[level]
        return pl.ds(pl.multiple_of(self.base[level] + n * size, 8), size)

    def send(self, level):
        self.copies = []
        for d in range(1, self.counts[level]):
            there = (self.index[level] + d) % self.counts[level]
            self.copies.append(self.remote(
                self.buf.at[self.rows(level, there)], self.slots[level].at[d - 1],
                self.sems[0].at[level, d - 1], self.sems[1].at[level, d - 1], self.peers[level](d)))
            self.copies[-1].start()

    def add(self, level):
        for copy in self.copies:
            copy.wait()
        mine = self.rows(level, self.index[level])
        value = self.buf[mine, :]
        for d in range(1, self.counts[level]):
            value = value + self.slots[level][d - 1]
        if level == 2:
            self.out[mine, :] = value
        else:
            self.buf[mine, :] = value

    def share(self, level, start=True):
        mine = self.out.at[self.rows(level, self.index[level])]
        self.copies = []
        for d in range(1, self.counts[level]):
            self.copies.append(self.remote(
                mine, mine, self.sems[2].at[level, d - 1], self.sems[3].at[level, d - 1], self.peers[level](d)))
        if start:
            self.start()

    def start(self):
        for copy in self.copies:
            copy.start()

    def wait(self):
        for copy in self.copies:
            copy.wait()


def whole_kernel(groups, spans, pieces, scale, rec, tri, op, gram_out, cross_out, work, mid, inverses, ext, own, left, right, after, acc,
                eleft, eright, eafter, dgram, dcross, wgram, wcross,
                local_sem, xs, xr, zs, zr, es, er, *reduce_refs):
    grp, span = lax.axis_index("grp"), lax.axis_index("span")
    pairs = spans // 2
    h, q = span % 2, span // 2
    core, y = grp % 2, grp // 2
    plane, place = groups, y * 2 + h
    at, count = grp * pairs + q, groups * pairs
    has_prev, has_next = at > 0, at < count - 1

    def device(pair, side):
        pair = (pair + count) % count
        return (pair // pairs, (pair % pairs) * 2 + side)

    def plane_peer(d):
        there = (place + d) % plane
        return ((there // 2) * 2 + core, q * 2 + there % 2)

    def line_peer(d):
        return (grp, ((q + d) % pairs) * 2 + h)

    core_peer = (y * 2 + 1 - core, span)
    partner = (grp, q * 2 + 1 - h)
    z_to = device(at - 1 + 2 * h, h)
    sends_z = jnp.where(h == 0, at, count - 1 - at) > 0
    gets_z = jnp.where(h == 0, count - 1 - at, at) > 0

    own_copy = pltpu.make_async_copy(
        rec.at[:, pl.ds(h * HALF, HALF), :], ext.at[pl.ds(1 + 7 * h, 4), pl.ds(0, HALF), :], local_sem.at[0])
    own_extra = pltpu.make_async_copy(
        rec.at[:, pl.ds((1 - h) * HALF, 8), :], ext.at[pl.ds(1 + 6 * h, 4), pl.ds(HALF, 8), :], local_sem.at[1])
    own_copy.start()
    own_extra.start()
    edge = (at * 2 + h == 0) | (at * 2 + h == 2 * count - 1)
    full_copy = pltpu.make_async_copy(rec, own.at[pl.ds(0, LAGS)], local_sem.at[2])

    @pl.when(edge)
    def _():
        full_copy.start()

    barrier = pltpu.get_barrier_semaphore()

    def greet(to):
        pl.semaphore_signal(barrier, inc=1, device_id=to, device_id_type=MESH)

    greet(core_peer)
    for d in range(1, plane):
        greet(plane_peer(d))
    for d in range(1, pairs):
        greet(line_peer(d))

    @pl.when(has_prev)
    def _():
        greet(device(at - 1, h))

    @pl.when(has_next)
    def _():
        greet(device(at + 1, h))

    @pl.when((h == 0) & has_prev)
    def _():
        greet(device(at - 1, 1))

    @pl.when((h == 1) & has_next)
    def _():
        greet(device(at + 1, 0))

    pl.semaphore_wait(
        barrier, plane + pairs - 1
        + jnp.where(has_prev, 1, 0) + jnp.where(has_next, 1, 0)
        + jnp.where((h == 0) & has_prev, 1, 0) + jnp.where((h == 1) & has_next, 1, 0))

    def remote(src, dst, send, recv, to):
        return pltpu.make_async_remote_copy(
            src_ref=src, dst_ref=dst, send_sem=send, recv_sem=recv, device_id=to, device_id_type=MESH)

    def x_copy(c):
        return remote(
            rec.at[:, pl.ds((1 - h) * HALF + c * UNIT, UNIT), :],
            ext.at[pl.ds(4 + h, 4), pl.ds(c * UNIT, UNIT), :], xs.at[c], xr.at[c], partner)

    def z_copy(c):
        return remote(
            rec.at[pl.ds(h, 3), pl.ds(h * HALF + c * UNIT, UNIT), :],
            ext.at[pl.ds(9 - 8 * h, 3), pl.ds(c * UNIT, UNIT), :], zs.at[c], zr.at[c], z_to)

    x_extra = remote(
        rec.at[:, pl.ds(h * HALF, 8), :], ext.at[pl.ds(3 + 2 * h, 4), pl.ds(HALF, 8), :],
        es.at[0], er.at[0], partner)
    z_extra = remote(
        rec.at[pl.ds(h, 3), pl.ds((1 - h) * HALF, 8), :], ext.at[pl.ds(9 - 9 * h, 3), pl.ds(HALF, 8), :],
        es.at[1], er.at[1], z_to)
    d_extra = remote(
        rec.at[pl.ds(0, 1), pl.ds(0, 8), :], ext.at[pl.ds(11, 1), pl.ds(HALF, 8), :],
        es.at[2], er.at[2], device(at - 1, 1))

    x_extra.start()
    for c in reversed(range(CHUNKS)):
        x_copy(c).start()

    @pl.when(sends_z)
    def _():
        z_extra.start()
        for c in reversed(range(CHUNKS)):
            z_copy(c).start()

    @pl.when((h == 0) & has_prev)
    def _():
        d_extra.start()

    @pl.when(jnp.logical_not(gets_z))
    def _():
        ext[pl.ds(9 - 8 * h, 3), pl.ds(0, HALF), :] = jnp.zeros((3, HALF, UNIT), jnp.float32)

    acc[...] = jnp.zeros(acc.shape, jnp.float32)

    @pl.when(edge)
    def _():
        last = jnp.where(at > 0, 1, 0)
        own[LAGS, pl.ds(0, 8), :] = jnp.zeros((8, UNIT), jnp.float32)
        full_copy.wait()
        parts = DELAY // UNIT

        def unit(t, carry):
            block, row = t // parts, (t % parts) * UNIT
            rows = own[last + block, pl.ds(pl.multiple_of(row, UNIT), UNIT), :]
            more = t + 1
            tail = own[last + more // parts, pl.ds(pl.multiple_of((more % parts) * UNIT, UNIT), 8), :]
            prepare(jnp.concatenate([rows, tail], 0), pl.multiple_of(t * UNIT, UNIT), eleft, eright, eafter)
            return carry
        lax.fori_loop(0, 3 * parts, unit, 0)

        def excess(t, carry):
            i, j = t // 3, t % 3
            dgram[t] = quarters(product(eleft, i * DELAY, eright, j * DELAY, DELAY))
            dcross[t] = quarters(product(eleft, i * DELAY, eafter, j * DELAY, DELAY))
            return carry
        lax.fori_loop(0, 9, excess, 0)

        sub = lax.broadcasted_iota(jnp.int32, (8, UNIT), 0)

        def pick(block, start, row):
            rows = jnp.where(sub == row, own[block, pl.ds(pl.multiple_of(start, 8), 8), :], 0.0)
            line = jnp.sum(rows, axis=0, keepdims=True)
            return jnp.where(sub == 0, jnp.broadcast_to(line, (8, UNIT)), 0.0)
        ends = jnp.concatenate([pick(k, last * (DELAY - 8), last * 7) for k in range(LAGS)], 1)
        lead = jnp.concatenate([pick(l + 1, 0, 0) for l in range(LAGS)], 1)
        lead = lead * last.astype(jnp.float32)
        wgram[...] = (0.5 + last.astype(jnp.float32)) * contract(ends, ends, ((0,), (0,)), HIGH)
        wcross[...] = contract(ends, lead, ((0,), (0,)), HIGH)

    own_copy.wait()
    own_extra.wait()
    x_extra.wait_recv()

    @pl.when(gets_z)
    def _():
        z_extra.wait_recv()

    @pl.when((h == 1) & has_next)
    def _():
        d_extra.wait_recv()

    @pl.when((h == 0) & jnp.logical_not(has_next))
    def _():
        ext[pl.ds(9, 3), pl.ds(HALF, 8), :] = jnp.zeros((3, 8, UNIT), jnp.float32)

    @pl.when((h == 1) & jnp.logical_not(has_prev))
    def _():
        ext[pl.ds(0, 4), pl.ds(HALF, 8), :] = jnp.zeros((4, 8, UNIT), jnp.float32)

    @pl.when((h == 1) & jnp.logical_not(has_next))
    def _():
        ext[pl.ds(11, 1), pl.ds(HALF, 8), :] = jnp.zeros((1, 8, UNIT), jnp.float32)

    def load(c):
        def unit(t, base):
            e = base + t
            prepare(ext[e + 1, pl.ds(pl.multiple_of(c * UNIT, UNIT), UNIT + 8), :],
                    pl.multiple_of(e * UNIT, UNIT), left, right, after)
            return base
        lax.fori_loop(0, 4, unit, 7 * h)
        x_copy(c).wait_recv()

        @pl.when(gets_z)
        def _():
            z_copy(c).wait_recv()
        lax.fori_loop(0, 7, unit, 4 * (1 - h))

    def gram_lags():
        def lag(p, carry):
            a = h * (3 - p) * UNIT
            acc[p] += product(left, a, right, a + p * UNIT, 8 * UNIT)
            return carry
        lax.fori_loop(0, LAGS, lag, 0)

    def cross_lags():
        def lag(p, carry):
            a = h * (3 - p) * UNIT
            b = a + p * UNIT
            acc[LAGS + p] += product(left, a, after, b, 8 * UNIT)
            acc[2 * LAGS + p] += product(left, b, after, a, 8 * UNIT)
            return carry
        lax.fori_loop(0, LAGS, lag, 0)

    def chunk(step, carry):
        load(CHUNKS - 1 - step)
        gram_lags()
        cross_lags()
        return carry
    lax.fori_loop(0, CHUNKS - 1, chunk, 0)
    load(0)
    gram_lags()

    def term(n, k, l):
        if n < len(GRAM):
            return quarters(acc[l - k])
        return quarters(acc[LAGS + l - k] if l >= k else acc[2 * LAGS + k - l])

    blocks = GRAM + CROSS
    half = len(reduce_refs) // 2
    peers = (lambda d: core_peer, plane_peer, line_peer)
    gram, cross = (
        Total(remote, core, place, q, plane, pairs, piece, peers, (refs[0], out) + refs[1:])
        for piece, out, refs in zip(pieces, (gram_out, cross_out), (reduce_refs[:half], reduce_refs[half:])))

    def gather(total, numbers):
        @pl.when(jnp.logical_not(edge))
        def _():
            for m in range(-LAGS + 1, LAGS):
                which = [n for n in numbers if blocks[n][1] - blocks[n][0] == m]
                if which:
                    value = term(which[0], *blocks[which[0]])
                    for n in which:
                        total.buf[pl.ds((n - numbers[0]) * UNIT, UNIT), :] = value

        @pl.when(edge)
        def _():
            last = jnp.where(at > 0, 1, 0).astype(jnp.float32)
            for n in numbers:
                k, l = blocks[n]
                m = l - k
                value = term(n, k, l)
                less, ends = (dgram, wgram) if n < len(GRAM) else (dcross, wcross)
                for i in range(max(0, -m), min(2, 2 - m) + 1):
                    value = value - less[3 * i + i + m] * ((1.0 - last) if i < k else last)
                value = value - ends[pl.ds(k * UNIT, UNIT), pl.ds(l * UNIT, UNIT)]
                total.buf[pl.ds((n - numbers[0]) * UNIT, UNIT), :] = value
        used, size = len(numbers) * UNIT, total.buf.shape[0]
        if size > used:
            total.buf[pl.ds(used, size - used), :] = jnp.zeros((size - used, UNIT), jnp.float32)

    gather(gram, list(range(len(GRAM))))
    gram.send(0)
    gram.add(0)
    gram.send(1)
    cross_lags()
    gather(cross, list(range(len(GRAM), NB)))
    cross.send(0)
    cross.add(0)
    gram.add(1)
    gram.send(2)
    cross.send(1)
    gram.add(2)
    gram.share(2)
    cross.add(1)
    cross.send(2)
    gram.wait()
    gram.share(1)
    cross.add(2)
    cross.share(2)
    gram.wait()
    gram.share(0)
    cross.wait()
    cross.share(1)
    gram.wait()

    solve = Solve(scale, gram_out, cross_out, tri, op, work, mid, inverses)
    solve.load()

    solve.step(0)
    solve.invert(0)
    cross.wait()
    cross.share(0)
    solve.step(1)
    solve.invert(1)
    cross.wait()
    solve.second_half()

    x_extra.wait_send()
    for c in range(CHUNKS):
        x_copy(c).wait_send()

    @pl.when(sends_z)
    def _():
        z_extra.wait_send()
        for c in range(CHUNKS):
            z_copy(c).wait_send()

    @pl.when((h == 0) & has_prev)
    def _():
        d_extra.wait_send()


def on_device(record):
    count, comps = record.shape
    groups, spans = lax.axis_size("grp"), lax.axis_size("span")
    devices = groups * spans
    lead = (LAGS - 1) * DELAY + 1
    last_row = count * devices - lead
    pairs = spans // 2
    pieces = [-(-n * UNIT // (devices * 8)) * 8 for n in (len(GRAM), len(CROSS))]
    dma = pltpu.SemaphoreType.DMA
    f32, bf16 = jnp.float32, jnp.bfloat16
    vmem = pl.BlockSpec(memory_space=pltpu.VMEM)
    size = LAGS * comps
    return pl.pallas_call(
        functools.partial(whole_kernel, groups, spans, pieces, 1.0 / last_row),
        out_shape=(jax.ShapeDtypeStruct((size, size), f32),) * 2,
        in_specs=[pl.BlockSpec(memory_space=pl.ANY)], out_specs=(vmem, vmem),
        scratch_shapes=[
            *(pltpu.VMEM((piece * devices, UNIT), f32) for piece in pieces),
            *(pltpu.VMEM((size, size), f32),) * 3,
            pltpu.VMEM((12, HALF + 8, UNIT), f32),
            pltpu.VMEM((LAGS + 1, DELAY, UNIT), f32),
            pltpu.VMEM((2 * UNIT, 11 * UNIT), bf16),
            pltpu.VMEM((11 * UNIT, 2 * UNIT), bf16),
            pltpu.VMEM((11 * UNIT, 2 * UNIT), bf16),
            pltpu.VMEM((3 * LAGS, 2 * UNIT, 2 * UNIT), f32),
            pltpu.VMEM((2 * UNIT, 3 * DELAY), bf16),
            pltpu.VMEM((3 * DELAY, 2 * UNIT), bf16),
            pltpu.VMEM((3 * DELAY, 2 * UNIT), bf16),
            pltpu.VMEM((9, UNIT, UNIT), f32),
            pltpu.VMEM((9, UNIT, UNIT), f32),
            pltpu.VMEM((LAGS * UNIT, LAGS * UNIT), f32),
            pltpu.VMEM((LAGS * UNIT, LAGS * UNIT), f32),
            dma((3,)), dma((CHUNKS,)), dma((CHUNKS,)), dma((CHUNKS,)), dma((CHUNKS,)), dma((3,)), dma((3,)),
            *(ref for piece in pieces for ref in (
                pltpu.VMEM((piece * devices, UNIT), f32),
                pltpu.VMEM((1, piece * devices // 2, UNIT), f32),
                pltpu.VMEM((groups - 1, pairs * piece, UNIT), f32),
                pltpu.VMEM((pairs - 1, piece, UNIT), f32),
                *(dma((3, max(groups, pairs) - 1)),) * 4)),
        ],
        compiler_params=pltpu.CompilerParams(
            collective_id=0, has_side_effects=True, vmem_limit_bytes=56 << 20),
    )(record.reshape(LAGS, DELAY, comps))


def solution(mesh):
    placed = (P(AXES, None),)
    return jax.shard_map(
        on_device, mesh=mesh, in_specs=placed, out_specs=(P(), P()), check_vma=False
    )
```

```python
import functools

import jax
import jax.numpy as jnp
from jax import lax
from jax.experimental import pallas as pl
from jax.experimental.pallas import tpu as pltpu
from jax.sharding import PartitionSpec as P

LAGS = 4
DELAY = 1024
AXES = ("grp", "span")
HIGH = lax.Precision.HIGHEST
MESH = pl.DeviceIdType.MESH
UNIT = 128
HALF = DELAY // 2
CHUNKS = HALF // UNIT
GRAM = [(k, l) for k in range(LAGS) for l in range(k, LAGS)]
CROSS = [(k, l) for k in range(LAGS) for l in range(LAGS)]
NB = len(GRAM) + len(CROSS)


def contract(left, right, dims, precision=None):
    return lax.dot_general(
        left, right, (dims, ((), ())), precision=precision,
        preferred_element_type=jnp.float32,
    )


def factor(block):
    n = block.shape[0]
    groups = n // 8
    lane = lax.broadcasted_iota(jnp.int32, (8, n), 1)
    sub = lax.broadcasted_iota(jnp.int32, (8, n), 0)
    a = [block[8 * g:8 * g + 8, :] for g in range(groups)]
    b = [jnp.where(lane == sub + 8 * g, 1.0, 0.0) for g in range(groups)]

    def column(x, k):
        return jnp.broadcast_to(x[:, k:k + 1], (8, n))

    def line(x, i):
        return jnp.broadcast_to(x[i:i + 1, :], (8, n))

    def total(terms):
        while len(terms) > 2:
            terms = [terms[0] + terms[1]] + terms[2:] if len(terms) % 2 else [
                terms[i] + terms[i + 1] for i in range(0, len(terms), 2)]
        return terms[0] + terms[1]

    def stack(rows):
        value = rows[0]
        for i in range(1, 8):
            value = jnp.where(sub == i, rows[i], value)
        return value

    for g in range(groups):
        cols = [column(a[g], 8 * g + j) for j in range(8)]
        s = [[line(cols[j], i) for j in range(i + 1)] for i in range(8)]
        rows = [line(a[g], i) for i in range(8)]
        lines = [line(b[g], i) for i in range(8)]
        inverse = []
        for r in range(8):
            inverse.append(1.0 / s[r][r])
            factors = [s[i][r] * inverse[r] for i in range(r + 1, 8)]
            for i in range(r + 1, 8):
                for j in range(r + 1, i + 1):
                    s[i][j] = s[i][j] - factors[i - r - 1] * s[j][r]
            for i in range(r + 1, 8):
                s[i][r] = factors[i - r - 1]
                rows[i] = rows[i] - s[i][r] * rows[r]
                lines[i] = lines[i] - s[i][r] * lines[r]
        scale = lax.rsqrt(stack([s[r][r] for r in range(8)]))
        left, right = list(rows), list(lines)
        for r in reversed(range(8)):
            left[r] = rows[r] * inverse[r]
            right[r] = lines[r] * inverse[r]
            for i in reversed(range(r + 1, 8)):
                left[r] = left[r] - s[i][r] * left[i]
                right[r] = right[r] - s[i][r] * right[i]
        for h in range(g + 1, groups):
            c = [column(a[h], 8 * g + j) for j in range(8)]
            a[h] = a[h] - total([c[j] * left[j] for j in reversed(range(8))])
            b[h] = b[h] - total([c[j] * right[j] for j in reversed(range(8))])
        a[g] = jnp.where(lane >= sub + 8 * g, stack(rows) * scale, 0.0)
        b[g] = stack(lines) * scale
    return jnp.concatenate(a, 0), jnp.concatenate(b, 0)


class Solve:
    def __init__(self, scale, gram, cross, tri, op, work, mid, inverse):
        self.scale, self.gram, self.cross, self.tri, self.op = scale, gram, cross, tri, op
        self.work, self.mid, self.inverse = work, mid, inverse

    def load(self):
        for n, (i, j) in enumerate(GRAM):
            self.work[cut(i), cut(j)] = self.gram[cut(n), :] * self.scale
        self.inverse[...] = jnp.zeros(self.inverse.shape, jnp.float32)

    def load_cross(self):
        for n, (i, j) in enumerate(CROSS):
            self.mid[cut(i), cut(j)] = self.cross[cut(n), :] * self.scale

    def step(self, k):
        work, rest = self.work, LAGS - k - 1
        upper, inverse = factor(work[cut(k), cut(k)])
        work[cut(k), cut(k)] = upper
        self.inverse[cut(k), cut(k)] = inverse
        if rest:
            work[cut(k), cut(k + 1, rest)] = contract(
                inverse, work[cut(k), cut(k + 1, rest)], ((1,), (0,)), HIGH)
        for j in range(k + 1, LAGS):
            to = (cut(j), cut(j, LAGS - j))
            work[to] = work[to] - contract(work[cut(k), cut(j)], work[cut(k), to[1]], ((0,), (0,)), HIGH)

    def invert(self, k):
        inverse = self.inverse
        if k:
            inverse[cut(k), cut(0, k)] = contract(
                inverse[cut(k), cut(k)], inverse[cut(k), cut(0, k)], ((1,), (0,)), HIGH)
        if k < LAGS - 1:
            to = (cut(k + 1, LAGS - k - 1), cut(0, k + 1))
            inverse[to] = inverse[to] - contract(
                self.work[cut(k), to[0]], inverse[cut(k), to[1]], ((0,), (0,)), HIGH)

    def apply(self, k):
        mid = self.mid
        mid[cut(k), :] = contract(self.inverse[cut(k), cut(k)], mid[cut(k), :], ((1,), (0,)), HIGH)
        if k < LAGS - 1:
            below = cut(k + 1, LAGS - k - 1)
            mid[below, :] = mid[below, :] - contract(
                self.work[cut(k), below], mid[cut(k), :], ((0,), (0,)), HIGH)

    def operate(self, rows, cols, depth):
        self.op[rows, cols] = contract(
            self.mid[rows, cut(0, depth)], self.inverse[cols, cut(0, depth)], ((1,), (1,)), HIGH)

    def triangle(self):
        for i in range(LAGS):
            self.tri[cut(i), cut(i, LAGS - i)] = self.work[cut(i), cut(i, LAGS - i)]
            if i:
                self.tri[cut(i), cut(0, i)] = jnp.zeros((UNIT, i * UNIT), jnp.float32)

    def second_half(self):
        self.load_cross()
        self.step(2)
        self.apply(0)
        self.apply(1)
        self.step(3)
        self.apply(2)
        self.invert(2)
        self.operate(cut(0, 3), cut(0, 3), 3)
        self.apply(3)
        self.invert(3)
        self.operate(cut(0, 3), cut(3), 4)
        self.operate(cut(3), cut(0, 4), 4)
        self.triangle()


def cut(n, count=1):
    return pl.ds(n * UNIT, count * UNIT)


def halves(x):
    spread = x * 65537.0
    high = spread - (spread - x)
    return high.astype(jnp.bfloat16), (x - high).astype(jnp.bfloat16)


def quarters(x):
    n = x.shape[0] // 2
    return (x[:n, :n] + x[:n, n:]) + (x[n:, :n] + x[n:, n:])


def prepare(window, at, left, right, after):
    cols = pl.ds(at, UNIT)
    rows = window[:UNIT]
    high, low = halves(rows)
    right[cols, pl.ds(0, UNIT)] = high
    right[cols, pl.ds(UNIT, UNIT)] = low
    high, low = halves(rows.T)
    left[pl.ds(0, UNIT), cols] = high
    left[pl.ds(UNIT, UNIT), cols] = low
    high, low = halves(pltpu.roll(window, window.shape[0] - 1, 0)[:UNIT])
    after[cols, pl.ds(0, UNIT)] = high
    after[cols, pl.ds(UNIT, UNIT)] = low


def product(left, lcol, right, rrow, depth):
    lcol = pl.multiple_of(lcol, UNIT)
    rrow = pl.multiple_of(rrow, UNIT)
    return jnp.dot(left[:, pl.ds(lcol, depth)], right[pl.ds(rrow, depth), :],
                   preferred_element_type=jnp.float32)


class Total:
    def __init__(self, remote, core, place, q, plane, pairs, piece, peers, refs):
        self.buf, self.out, self.slots = refs[0], refs[1], refs[2:5]
        self.sems = refs[5:]
        self.remote, self.piece = remote, piece
        self.sizes = (plane * pairs * piece, pairs * piece, piece)
        self.index, self.counts, self.peers = (core, place, q), (2, plane, pairs), peers
        self.base = [0]
        for size, index in zip(self.sizes, self.index):
            self.base.append(self.base[-1] + index * size)
        self.copies = []

    def rows(self, level, n):
        size = self.sizes[level]
        return pl.ds(pl.multiple_of(self.base[level] + n * size, 8), size)

    def send(self, level):
        self.copies = []
        for d in range(1, self.counts[level]):
            there = (self.index[level] + d) % self.counts[level]
            self.copies.append(self.remote(
                self.buf.at[self.rows(level, there)], self.slots[level].at[d - 1],
                self.sems[0].at[level, d - 1], self.sems[1].at[level, d - 1], self.peers[level](d)))
            self.copies[-1].start()

    def add(self, level):
        for copy in self.copies:
            copy.wait()
        mine = self.rows(level, self.index[level])
        value = self.buf[mine, :]
        for d in range(1, self.counts[level]):
            value = value + self.slots[level][d - 1]
        if level == 2:
            self.out[mine, :] = value
        else:
            self.buf[mine, :] = value

    def share(self, level, start=True):
        mine = self.out.at[self.rows(level, self.index[level])]
        self.copies = []
        for d in range(1, self.counts[level]):
            self.copies.append(self.remote(
                mine, mine, self.sems[2].at[level, d - 1], self.sems[3].at[level, d - 1], self.peers[level](d)))
        if start:
            self.start()

    def start(self):
        for copy in self.copies:
            copy.start()

    def wait(self):
        for copy in self.copies:
            copy.wait()


def whole_kernel(groups, spans, pieces, scale, rec, tri, op, gram_out, cross_out, work, mid, inverses, ext, own, left, right, after, acc,
                eleft, eright, eafter, dgram, dcross, wgram, wcross,
                local_sem, xs, xr, zs, zr, es, er, *reduce_refs):
    grp, span = lax.axis_index("grp"), lax.axis_index("span")
    pairs = spans // 2
    h, q = span % 2, span // 2
    core, y = grp % 2, grp // 2
    plane, place = groups, y * 2 + h
    at, count = grp * pairs + q, groups * pairs
    has_prev, has_next = at > 0, at < count - 1

    def device(pair, side):
        pair = (pair + count) % count
        return (pair // pairs, (pair % pairs) * 2 + side)

    def plane_peer(d):
        there = (place + d) % plane
        return ((there // 2) * 2 + core, q * 2 + there % 2)

    def line_peer(d):
        return (grp, ((q + d) % pairs) * 2 + h)

    core_peer = (y * 2 + 1 - core, span)
    partner = (grp, q * 2 + 1 - h)
    z_to = device(at - 1 + 2 * h, h)
    sends_z = jnp.where(h == 0, at, count - 1 - at) > 0
    gets_z = jnp.where(h == 0, count - 1 - at, at) > 0

    own_copy = pltpu.make_async_copy(
        rec.at[:, pl.ds(h * HALF, HALF), :], ext.at[pl.ds(1 + 7 * h, 4), pl.ds(0, HALF), :], local_sem.at[0])
    own_extra = pltpu.make_async_copy(
        rec.at[:, pl.ds((1 - h) * HALF, 8), :], ext.at[pl.ds(1 + 6 * h, 4), pl.ds(HALF, 8), :], local_sem.at[1])
    own_copy.start()
    own_extra.start()
    edge = (at * 2 + h == 0) | (at * 2 + h == 2 * count - 1)
    full_copy = pltpu.make_async_copy(rec, own.at[pl.ds(0, LAGS)], local_sem.at[2])

    @pl.when(edge)
    def _():
        full_copy.start()

    barrier = pltpu.get_barrier_semaphore()

    def greet(to):
        pl.semaphore_signal(barrier, inc=1, device_id=to, device_id_type=MESH)

    greet(core_peer)
    for d in range(1, plane):
        greet(plane_peer(d))
    for d in range(1, pairs):
        greet(line_peer(d))

    @pl.when(has_prev)
    def _():
        greet(device(at - 1, h))

    @pl.when(has_next)
    def _():
        greet(device(at + 1, h))

    @pl.when((h == 0) & has_prev)
    def _():
        greet(device(at - 1, 1))

    @pl.when((h == 1) & has_next)
    def _():
        greet(device(at + 1, 0))

    pl.semaphore_wait(
        barrier, plane + pairs - 1
        + jnp.where(has_prev, 1, 0) + jnp.where(has_next, 1, 0)
        + jnp.where((h == 0) & has_prev, 1, 0) + jnp.where((h == 1) & has_next, 1, 0))

    def remote(src, dst, send, recv, to):
        return pltpu.make_async_remote_copy(
            src_ref=src, dst_ref=dst, send_sem=send, recv_sem=recv, device_id=to, device_id_type=MESH)

    def x_copy(c):
        return remote(
            rec.at[:, pl.ds((1 - h) * HALF + c * UNIT, UNIT), :],
            ext.at[pl.ds(4 + h, 4), pl.ds(c * UNIT, UNIT), :], xs.at[c], xr.at[c], partner)

    def z_copy(c):
        return remote(
            rec.at[pl.ds(h, 3), pl.ds(h * HALF + c * UNIT, UNIT), :],
            ext.at[pl.ds(9 - 8 * h, 3), pl.ds(c * UNIT, UNIT), :], zs.at[c], zr.at[c], z_to)

    x_extra = remote(
        rec.at[:, pl.ds(h * HALF, 8), :], ext.at[pl.ds(3 + 2 * h, 4), pl.ds(HALF, 8), :],
        es.at[0], er.at[0], partner)
    z_extra = remote(
        rec.at[pl.ds(h, 3), pl.ds((1 - h) * HALF, 8), :], ext.at[pl.ds(9 - 9 * h, 3), pl.ds(HALF, 8), :],
        es.at[1], er.at[1], z_to)
    d_extra = remote(
        rec.at[pl.ds(0, 1), pl.ds(0, 8), :], ext.at[pl.ds(11, 1), pl.ds(HALF, 8), :],
        es.at[2], er.at[2], device(at - 1, 1))

    x_extra.start()
    for c in reversed(range(CHUNKS)):
        x_copy(c).start()

    @pl.when(sends_z)
    def _():
        z_extra.start()
        for c in reversed(range(CHUNKS)):
            z_copy(c).start()

    @pl.when((h == 0) & has_prev)
    def _():
        d_extra.start()

    @pl.when(jnp.logical_not(gets_z))
    def _():
        ext[pl.ds(9 - 8 * h, 3), pl.ds(0, HALF), :] = jnp.zeros((3, HALF, UNIT), jnp.float32)

    acc[...] = jnp.zeros(acc.shape, jnp.float32)

    @pl.when(edge)
    def _():
        last = jnp.where(at > 0, 1, 0)
        own[LAGS, pl.ds(0, 8), :] = jnp.zeros((8, UNIT), jnp.float32)
        full_copy.wait()
        parts = DELAY // UNIT

        def unit(t, carry):
            block, row = t // parts, (t % parts) * UNIT
            rows = own[last + block, pl.ds(pl.multiple_of(row, UNIT), UNIT), :]
            more = t + 1
            tail = own[last + more // parts, pl.ds(pl.multiple_of((more % parts) * UNIT, UNIT), 8), :]
            prepare(jnp.concatenate([rows, tail], 0), pl.multiple_of(t * UNIT, UNIT), eleft, eright, eafter)
            return carry
        lax.fori_loop(0, 3 * parts, unit, 0)

        def excess(t, carry):
            i, j = t // 3, t % 3
            dgram[t] = quarters(product(eleft, i * DELAY, eright, j * DELAY, DELAY))
            dcross[t] = quarters(product(eleft, i * DELAY, eafter, j * DELAY, DELAY))
            return carry
        lax.fori_loop(0, 9, excess, 0)

        sub = lax.broadcasted_iota(jnp.int32, (8, UNIT), 0)

        def pick(block, start, row):
            rows = jnp.where(sub == row, own[block, pl.ds(pl.multiple_of(start, 8), 8), :], 0.0)
            line = jnp.sum(rows, axis=0, keepdims=True)
            return jnp.where(sub == 0, jnp.broadcast_to(line, (8, UNIT)), 0.0)
        ends = jnp.concatenate([pick(k, last * (DELAY - 8), last * 7) for k in range(LAGS)], 1)
        lead = jnp.concatenate([pick(l + 1, 0, 0) for l in range(LAGS)], 1)
        lead = lead * last.astype(jnp.float32)
        wgram[...] = (0.5 + last.astype(jnp.float32)) * contract(ends, ends, ((0,), (0,)), HIGH)
        wcross[...] = contract(ends, lead, ((0,), (0,)), HIGH)

    own_copy.wait()
    own_extra.wait()
    x_extra.wait_recv()

    @pl.when(gets_z)
    def _():
        z_extra.wait_recv()

    @pl.when((h == 1) & has_next)
    def _():
        d_extra.wait_recv()

    @pl.when((h == 0) & jnp.logical_not(has_next))
    def _():
        ext[pl.ds(9, 3), pl.ds(HALF, 8), :] = jnp.zeros((3, 8, UNIT), jnp.float32)

    @pl.when((h == 1) & jnp.logical_not(has_prev))
    def _():
        ext[pl.ds(0, 4), pl.ds(HALF, 8), :] = jnp.zeros((4, 8, UNIT), jnp.float32)

    @pl.when((h == 1) & jnp.logical_not(has_next))
    def _():
        ext[pl.ds(11, 1), pl.ds(HALF, 8), :] = jnp.zeros((1, 8, UNIT), jnp.float32)

    def load(c):
        def unit(t, base):
            e = base + t
            prepare(ext[e + 1, pl.ds(pl.multiple_of(c * UNIT, UNIT), UNIT + 8), :],
                    pl.multiple_of(e * UNIT, UNIT), left, right, after)
            return base
        lax.fori_loop(0, 4, unit, 7 * h)
        x_copy(c).wait_recv()

        @pl.when(gets_z)
        def _():
            z_copy(c).wait_recv()
        lax.fori_loop(0, 7, unit, 4 * (1 - h))

    def gram_lags():
        def lag(p, carry):
            a = h * (3 - p) * UNIT
            acc[p] += product(left, a, right, a + p * UNIT, 8 * UNIT)
            return carry
        lax.fori_loop(0, LAGS, lag, 0)

    def cross_lags():
        def lag(p, carry):
            a = h * (3 - p) * UNIT
            b = a + p * UNIT
            acc[LAGS + p] += product(left, a, after, b, 8 * UNIT)
            acc[2 * LAGS + p] += product(left, b, after, a, 8 * UNIT)
            return carry
        lax.fori_loop(0, LAGS, lag, 0)

    def chunk(step, carry):
        load(CHUNKS - 1 - step)
        gram_lags()
        cross_lags()
        return carry
    lax.fori_loop(0, CHUNKS - 1, chunk, 0)
    load(0)
    gram_lags()

    def term(n, k, l):
        if n < len(GRAM):
            return quarters(acc[l - k])
        return quarters(acc[LAGS + l - k] if l >= k else acc[2 * LAGS + k - l])

    blocks = GRAM + CROSS
    half = len(reduce_refs) // 2
    peers = (lambda d: core_peer, plane_peer, line_peer)
    gram, cross = (
        Total(remote, core, place, q, plane, pairs, piece, peers, (refs[0], out) + refs[1:])
        for piece, out, refs in zip(pieces, (gram_out, cross_out), (reduce_refs[:half], reduce_refs[half:])))

    def gather(total, numbers):
        @pl.when(jnp.logical_not(edge))
        def _():
            for m in range(-LAGS + 1, LAGS):
                which = [n for n in numbers if blocks[n][1] - blocks[n][0] == m]
                if which:
                    value = term(which[0], *blocks[which[0]])
                    for n in which:
                        total.buf[pl.ds((n - numbers[0]) * UNIT, UNIT), :] = value

        @pl.when(edge)
        def _():
            last = jnp.where(at > 0, 1, 0).astype(jnp.float32)
            for n in numbers:
                k, l = blocks[n]
                m = l - k
                value = term(n, k, l)
                less, ends = (dgram, wgram) if n < len(GRAM) else (dcross, wcross)
                for i in range(max(0, -m), min(2, 2 - m) + 1):
                    value = value - less[3 * i + i + m] * ((1.0 - last) if i < k else last)
                value = value - ends[pl.ds(k * UNIT, UNIT), pl.ds(l * UNIT, UNIT)]
                total.buf[pl.ds((n - numbers[0]) * UNIT, UNIT), :] = value
        used, size = len(numbers) * UNIT, total.buf.shape[0]
        if size > used:
            total.buf[pl.ds(used, size - used), :] = jnp.zeros((size - used, UNIT), jnp.float32)

    gather(gram, list(range(len(GRAM))))
    gram.send(0)
    gram.add(0)
    gram.send(1)
    cross_lags()
    gather(cross, list(range(len(GRAM), NB)))
    cross.send(0)
    cross.add(0)
    gram.add(1)
    gram.send(2)
    cross.send(1)
    gram.add(2)
    gram.share(2)
    cross.add(1)
    cross.send(2)
    gram.wait()
    gram.share(1)
    cross.add(2)
    cross.share(2)
    gram.wait()
    gram.share(0)
    cross.wait()
    cross.share(1)
    gram.wait()

    solve = Solve(scale, gram_out, cross_out, tri, op, work, mid, inverses)
    solve.load()

    solve.step(0)
    solve.invert(0)
    cross.wait()
    cross.share(0)
    solve.step(1)
    solve.invert(1)
    cross.wait()
    solve.second_half()

    x_extra.wait_send()
    for c in range(CHUNKS):
        x_copy(c).wait_send()

    @pl.when(sends_z)
    def _():
        z_extra.wait_send()
        for c in range(CHUNKS):
            z_copy(c).wait_send()

    @pl.when((h == 0) & has_prev)
    def _():
        d_extra.wait_send()


def on_device(record):
    count, comps = record.shape
    groups, spans = lax.axis_size("grp"), lax.axis_size("span")
    devices = groups * spans
    lead = (LAGS - 1) * DELAY + 1
    last_row = count * devices - lead
    pairs = spans // 2
    pieces = [-(-n * UNIT // (devices * 8)) * 8 for n in (len(GRAM), len(CROSS))]
    dma = pltpu.SemaphoreType.DMA
    f32, bf16 = jnp.float32, jnp.bfloat16
    vmem = pl.BlockSpec(memory_space=pltpu.VMEM)
    size = LAGS * comps
    return pl.pallas_call(
        functools.partial(whole_kernel, groups, spans, pieces, 1.0 / last_row),
        out_shape=(jax.ShapeDtypeStruct((size, size), f32),) * 2,
        in_specs=[pl.BlockSpec(memory_space=pl.ANY)], out_specs=(vmem, vmem),
        scratch_shapes=[
            *(pltpu.VMEM((piece * devices, UNIT), f32) for piece in pieces),
            *(pltpu.VMEM((size, size), f32),) * 3,
            pltpu.VMEM((12, HALF + 8, UNIT), f32),
            pltpu.VMEM((LAGS + 1, DELAY, UNIT), f32),
            pltpu.VMEM((2 * UNIT, 11 * UNIT), bf16),
            pltpu.VMEM((11 * UNIT, 2 * UNIT), bf16),
            pltpu.VMEM((11 * UNIT, 2 * UNIT), bf16),
            pltpu.VMEM((3 * LAGS, 2 * UNIT, 2 * UNIT), f32),
            pltpu.VMEM((2 * UNIT, 3 * DELAY), bf16),
            pltpu.VMEM((3 * DELAY, 2 * UNIT), bf16),
            pltpu.VMEM((3 * DELAY, 2 * UNIT), bf16),
            pltpu.VMEM((9, UNIT, UNIT), f32),
            pltpu.VMEM((9, UNIT, UNIT), f32),
            pltpu.VMEM((LAGS * UNIT, LAGS * UNIT), f32),
            pltpu.VMEM((LAGS * UNIT, LAGS * UNIT), f32),
            dma((3,)), dma((CHUNKS,)), dma((CHUNKS,)), dma((CHUNKS,)), dma((CHUNKS,)), dma((3,)), dma((3,)),
            *(ref for piece in pieces for ref in (
                pltpu.VMEM((piece * devices, UNIT), f32),
                pltpu.VMEM((1, piece * devices // 2, UNIT), f32),
                pltpu.VMEM((groups - 1, pairs * piece, UNIT), f32),
                pltpu.VMEM((pairs - 1, piece, UNIT), f32),
                *(dma((3, max(groups, pairs) - 1)),) * 4)),
        ],
        compiler_params=pltpu.CompilerParams(
            collective_id=0, has_side_effects=True, vmem_limit_bytes=56 << 20),
    )(record.reshape(LAGS, DELAY, comps))


def solution(mesh):
    placed = (P(AXES, None),)
    return jax.shard_map(
        on_device, mesh=mesh, in_specs=placed, out_specs=(P(), P()), check_vma=False
    )
```

```python
import functools

import jax
import jax.numpy as jnp
from jax import lax
from jax.experimental import pallas as pl
from jax.experimental.pallas import tpu as pltpu
from jax.sharding import PartitionSpec as P

LAGS = 4
DELAY = 1024
AXES = ("grp", "span")
HIGH = lax.Precision.HIGHEST
MESH = pl.DeviceIdType.MESH
UNIT = 128
HALF = DELAY // 2
CHUNKS = HALF // UNIT
GRAM = [(k, l) for k in range(LAGS) for l in range(k, LAGS)]
CROSS = [(k, l) for k in range(LAGS) for l in range(LAGS)]
NB = len(GRAM) + len(CROSS)


def contract(left, right, dims, precision=None):
    return lax.dot_general(
        left, right, (dims, ((), ())), precision=precision,
        preferred_element_type=jnp.float32,
    )


def factor(block):
    n = block.shape[0]
    groups = n // 8
    lane = lax.broadcasted_iota(jnp.int32, (8, n), 1)
    sub = lax.broadcasted_iota(jnp.int32, (8, n), 0)
    a = [block[8 * g:8 * g + 8, :] for g in range(groups)]
    b = [jnp.where(lane == sub + 8 * g, 1.0, 0.0) for g in range(groups)]

    def column(x, k):
        return jnp.broadcast_to(x[:, k:k + 1], (8, n))

    def line(x, i):
        return jnp.broadcast_to(x[i:i + 1, :], (8, n))

    def total(terms):
        while len(terms) > 2:
            terms = [terms[0] + terms[1]] + terms[2:] if len(terms) % 2 else [
                terms[i] + terms[i + 1] for i in range(0, len(terms), 2)]
        return terms[0] + terms[1]

    def stack(rows):
        value = rows[0]
        for i in range(1, 8):
            value = jnp.where(sub == i, rows[i], value)
        return value

    for g in range(groups):
        cols = [column(a[g], 8 * g + j) for j in range(8)]
        s = [[line(cols[j], i) for j in range(i + 1)] for i in range(8)]
        rows = [line(a[g], i) for i in range(8)]
        lines = [line(b[g], i) for i in range(8)]
        inverse, outs, others = [], [], []
        for r in range(8):
            inverse.append(1.0 / s[r][r])
            outs.append(rows[r])
            others.append(lines[r])
            pivot = [s[j][r] for j in range(8)]
            s[r][r + 1:] = pivot[r + 1:]
            for i in range(8):
                if i == r:
                    continue
                f = s[i][r] * inverse[r]
                for j in range(r + 1, i + 1 if i > r else 8):
                    s[i][j] = s[i][j] - f * pivot[j]
                rows[i] = rows[i] - f * rows[r]
                lines[i] = lines[i] - f * lines[r]
        scale = lax.rsqrt(stack([s[r][r] for r in range(8)]))
        left = [rows[r] * inverse[r] for r in range(8)]
        right = [lines[r] * inverse[r] for r in range(8)]
        for h in range(g + 1, groups):
            c = [column(a[h], 8 * g + j) for j in range(8)]
            a[h] = a[h] - total([c[j] * left[j] for j in reversed(range(8))])
            b[h] = b[h] - total([c[j] * right[j] for j in reversed(range(8))])
        a[g] = jnp.where(lane >= sub + 8 * g, stack(outs) * scale, 0.0)
        b[g] = stack(others) * scale
    return jnp.concatenate(a, 0), jnp.concatenate(b, 0)


class Solve:
    def __init__(self, scale, gram, cross, tri, op, work, mid, inverse):
        self.scale, self.gram, self.cross, self.tri, self.op = scale, gram, cross, tri, op
        self.work, self.mid, self.inverse = work, mid, inverse

    def load(self):
        for n, (i, j) in enumerate(GRAM):
            self.work[cut(i), cut(j)] = self.gram[cut(n), :] * self.scale
        self.inverse[...] = jnp.zeros(self.inverse.shape, jnp.float32)

    def load_cross(self):
        for n, (i, j) in enumerate(CROSS):
            self.mid[cut(i), cut(j)] = self.cross[cut(n), :] * self.scale

    def step(self, k):
        work, rest = self.work, LAGS - k - 1
        upper, inverse = factor(work[cut(k), cut(k)])
        work[cut(k), cut(k)] = upper
        self.inverse[cut(k), cut(k)] = inverse
        if rest:
            work[cut(k), cut(k + 1, rest)] = contract(
                inverse, work[cut(k), cut(k + 1, rest)], ((1,), (0,)), HIGH)
        for j in range(k + 1, LAGS):
            to = (cut(j), cut(j, LAGS - j))
            work[to] = work[to] - contract(work[cut(k), cut(j)], work[cut(k), to[1]], ((0,), (0,)), HIGH)

    def invert(self, k):
        inverse = self.inverse
        if k:
            inverse[cut(k), cut(0, k)] = contract(
                inverse[cut(k), cut(k)], inverse[cut(k), cut(0, k)], ((1,), (0,)), HIGH)
        if k < LAGS - 1:
            to = (cut(k + 1, LAGS - k - 1), cut(0, k + 1))
            inverse[to] = inverse[to] - contract(
                self.work[cut(k), to[0]], inverse[cut(k), to[1]], ((0,), (0,)), HIGH)

    def apply(self, k):
        mid = self.mid
        mid[cut(k), :] = contract(self.inverse[cut(k), cut(k)], mid[cut(k), :], ((1,), (0,)), HIGH)
        if k < LAGS - 1:
            below = cut(k + 1, LAGS - k - 1)
            mid[below, :] = mid[below, :] - contract(
                self.work[cut(k), below], mid[cut(k), :], ((0,), (0,)), HIGH)

    def operate(self, rows, cols, depth):
        self.op[rows, cols] = contract(
            self.mid[rows, cut(0, depth)], self.inverse[cols, cut(0, depth)], ((1,), (1,)), HIGH)

    def triangle(self):
        for i in range(LAGS):
            self.tri[cut(i), cut(i, LAGS - i)] = self.work[cut(i), cut(i, LAGS - i)]
            if i:
                self.tri[cut(i), cut(0, i)] = jnp.zeros((UNIT, i * UNIT), jnp.float32)

    def second_half(self):
        self.load_cross()
        self.step(2)
        self.apply(0)
        self.apply(1)
        self.step(3)
        self.apply(2)
        self.invert(2)
        self.operate(cut(0, 3), cut(0, 3), 3)
        self.apply(3)
        self.invert(3)
        self.operate(cut(0, 3), cut(3), 4)
        self.operate(cut(3), cut(0, 4), 4)
        self.triangle()


def cut(n, count=1):
    return pl.ds(n * UNIT, count * UNIT)


def halves(x):
    spread = x * 65537.0
    high = spread - (spread - x)
    return high.astype(jnp.bfloat16), (x - high).astype(jnp.bfloat16)


def quarters(x):
    n = x.shape[0] // 2
    return (x[:n, :n] + x[:n, n:]) + (x[n:, :n] + x[n:, n:])


def prepare(window, at, left, right, after):
    cols = pl.ds(at, UNIT)
    rows = window[:UNIT]
    high, low = halves(rows)
    right[cols, pl.ds(0, UNIT)] = high
    right[cols, pl.ds(UNIT, UNIT)] = low
    high, low = halves(rows.T)
    left[pl.ds(0, UNIT), cols] = high
    left[pl.ds(UNIT, UNIT), cols] = low
    high, low = halves(pltpu.roll(window, window.shape[0] - 1, 0)[:UNIT])
    after[cols, pl.ds(0, UNIT)] = high
    after[cols, pl.ds(UNIT, UNIT)] = low


def product(left, lcol, right, rrow, depth):
    lcol = pl.multiple_of(lcol, UNIT)
    rrow = pl.multiple_of(rrow, UNIT)
    return jnp.dot(left[:, pl.ds(lcol, depth)], right[pl.ds(rrow, depth), :],
                   preferred_element_type=jnp.float32)


class Total:
    def __init__(self, remote, core, place, q, plane, pairs, piece, peers, refs):
        self.buf, self.out, self.slots = refs[0], refs[1], refs[2:5]
        self.sems = refs[5:]
        self.remote, self.piece = remote, piece
        self.sizes = (plane * pairs * piece, pairs * piece, piece)
        self.index, self.counts, self.peers = (core, place, q), (2, plane, pairs), peers
        self.base = [0]
        for size, index in zip(self.sizes, self.index):
            self.base.append(self.base[-1] + index * size)
        self.copies = []

    def rows(self, level, n):
        size = self.sizes[level]
        return pl.ds(pl.multiple_of(self.base[level] + n * size, 8), size)

    def send(self, level):
        self.copies = []
        for d in range(1, self.counts[level]):
            there = (self.index[level] + d) % self.counts[level]
            self.copies.append(self.remote(
                self.buf.at[self.rows(level, there)], self.slots[level].at[d - 1],
                self.sems[0].at[level, d - 1], self.sems[1].at[level, d - 1], self.peers[level](d)))
            self.copies[-1].start()

    def add(self, level):
        for copy in self.copies:
            copy.wait()
        mine = self.rows(level, self.index[level])
        value = self.buf[mine, :]
        for d in range(1, self.counts[level]):
            value = value + self.slots[level][d - 1]
        if level == 2:
            self.out[mine, :] = value
        else:
            self.buf[mine, :] = value

    def share(self, level, start=True):
        mine = self.out.at[self.rows(level, self.index[level])]
        self.copies = []
        for d in range(1, self.counts[level]):
            self.copies.append(self.remote(
                mine, mine, self.sems[2].at[level, d - 1], self.sems[3].at[level, d - 1], self.peers[level](d)))
        if start:
            self.start()

    def start(self):
        for copy in self.copies:
            copy.start()

    def wait(self):
        for copy in self.copies:
            copy.wait()


def whole_kernel(groups, spans, pieces, scale, rec, tri, op, gram_out, cross_out, work, mid, inverses, ext, own, left, right, after, acc,
                eleft, eright, eafter, dgram, dcross, wgram, wcross,
                local_sem, xs, xr, zs, zr, es, er, *reduce_refs):
    grp, span = lax.axis_index("grp"), lax.axis_index("span")
    pairs = spans // 2
    h, q = span % 2, span // 2
    core, y = grp % 2, grp // 2
    plane, place = groups, y * 2 + h
    at, count = grp * pairs + q, groups * pairs
    has_prev, has_next = at > 0, at < count - 1

    def device(pair, side):
        pair = (pair + count) % count
        return (pair // pairs, (pair % pairs) * 2 + side)

    def plane_peer(d):
        there = (place + d) % plane
        return ((there // 2) * 2 + core, q * 2 + there % 2)

    def line_peer(d):
        return (grp, ((q + d) % pairs) * 2 + h)

    core_peer = (y * 2 + 1 - core, span)
    partner = (grp, q * 2 + 1 - h)
    z_to = device(at - 1 + 2 * h, h)
    sends_z = jnp.where(h == 0, at, count - 1 - at) > 0
    gets_z = jnp.where(h == 0, count - 1 - at, at) > 0

    own_copy = pltpu.make_async_copy(
        rec.at[:, pl.ds(h * HALF, HALF), :], ext.at[pl.ds(1 + 7 * h, 4), pl.ds(0, HALF), :], local_sem.at[0])
    own_extra = pltpu.make_async_copy(
        rec.at[:, pl.ds((1 - h) * HALF, 8), :], ext.at[pl.ds(1 + 6 * h, 4), pl.ds(HALF, 8), :], local_sem.at[1])
    own_copy.start()
    own_extra.start()
    edge = (at * 2 + h == 0) | (at * 2 + h == 2 * count - 1)
    full_copy = pltpu.make_async_copy(rec, own.at[pl.ds(0, LAGS)], local_sem.at[2])

    @pl.when(edge)
    def _():
        full_copy.start()

    barrier = pltpu.get_barrier_semaphore()

    def greet(to):
        pl.semaphore_signal(barrier, inc=1, device_id=to, device_id_type=MESH)

    greet(core_peer)
    for d in range(1, plane):
        greet(plane_peer(d))
    for d in range(1, pairs):
        greet(line_peer(d))

    @pl.when(has_prev)
    def _():
        greet(device(at - 1, h))

    @pl.when(has_next)
    def _():
        greet(device(at + 1, h))

    @pl.when((h == 0) & has_prev)
    def _():
        greet(device(at - 1, 1))

    @pl.when((h == 1) & has_next)
    def _():
        greet(device(at + 1, 0))

    pl.semaphore_wait(
        barrier, plane + pairs - 1
        + jnp.where(has_prev, 1, 0) + jnp.where(has_next, 1, 0)
        + jnp.where((h == 0) & has_prev, 1, 0) + jnp.where((h == 1) & has_next, 1, 0))

    def remote(src, dst, send, recv, to):
        return pltpu.make_async_remote_copy(
            src_ref=src, dst_ref=dst, send_sem=send, recv_sem=recv, device_id=to, device_id_type=MESH)

    def x_copy(c):
        return remote(
            rec.at[:, pl.ds((1 - h) * HALF + c * UNIT, UNIT), :],
            ext.at[pl.ds(4 + h, 4), pl.ds(c * UNIT, UNIT), :], xs.at[c], xr.at[c], partner)

    def z_copy(c):
        return remote(
            rec.at[pl.ds(h, 3), pl.ds(h * HALF + c * UNIT, UNIT), :],
            ext.at[pl.ds(9 - 8 * h, 3), pl.ds(c * UNIT, UNIT), :], zs.at[c], zr.at[c], z_to)

    x_extra = remote(
        rec.at[:, pl.ds(h * HALF, 8), :], ext.at[pl.ds(3 + 2 * h, 4), pl.ds(HALF, 8), :],
        es.at[0], er.at[0], partner)
    z_extra = remote(
        rec.at[pl.ds(h, 3), pl.ds((1 - h) * HALF, 8), :], ext.at[pl.ds(9 - 9 * h, 3), pl.ds(HALF, 8), :],
        es.at[1], er.at[1], z_to)
    d_extra = remote(
        rec.at[pl.ds(0, 1), pl.ds(0, 8), :], ext.at[pl.ds(11, 1), pl.ds(HALF, 8), :],
        es.at[2], er.at[2], device(at - 1, 1))

    x_extra.start()
    for c in reversed(range(CHUNKS)):
        x_copy(c).start()

    @pl.when(sends_z)
    def _():
        z_extra.start()
        for c in reversed(range(CHUNKS)):
            z_copy(c).start()

    @pl.when((h == 0) & has_prev)
    def _():
        d_extra.start()

    @pl.when(jnp.logical_not(gets_z))
    def _():
        ext[pl.ds(9 - 8 * h, 3), pl.ds(0, HALF), :] = jnp.zeros((3, HALF, UNIT), jnp.float32)

    acc[...] = jnp.zeros(acc.shape, jnp.float32)

    @pl.when(edge)
    def _():
        last = jnp.where(at > 0, 1, 0)
        own[LAGS, pl.ds(0, 8), :] = jnp.zeros((8, UNIT), jnp.float32)
        full_copy.wait()
        parts = DELAY // UNIT

        def unit(t, carry):
            block, row = t // parts, (t % parts) * UNIT
            rows = own[last + block, pl.ds(pl.multiple_of(row, UNIT), UNIT), :]
            more = t + 1
            tail = own[last + more // parts, pl.ds(pl.multiple_of((more % parts) * UNIT, UNIT), 8), :]
            prepare(jnp.concatenate([rows, tail], 0), pl.multiple_of(t * UNIT, UNIT), eleft, eright, eafter)
            return carry
        lax.fori_loop(0, 3 * parts, unit, 0)

        def excess(t, carry):
            i, j = t // 3, t % 3
            dgram[t] = quarters(product(eleft, i * DELAY, eright, j * DELAY, DELAY))
            dcross[t] = quarters(product(eleft, i * DELAY, eafter, j * DELAY, DELAY))
            return carry
        lax.fori_loop(0, 9, excess, 0)

        sub = lax.broadcasted_iota(jnp.int32, (8, UNIT), 0)

        def pick(block, start, row):
            rows = jnp.where(sub == row, own[block, pl.ds(pl.multiple_of(start, 8), 8), :], 0.0)
            line = jnp.sum(rows, axis=0, keepdims=True)
            return jnp.where(sub == 0, jnp.broadcast_to(line, (8, UNIT)), 0.0)
        ends = jnp.concatenate([pick(k, last * (DELAY - 8), last * 7) for k in range(LAGS)], 1)
        lead = jnp.concatenate([pick(l + 1, 0, 0) for l in range(LAGS)], 1)
        lead = lead * last.astype(jnp.float32)
        wgram[...] = (0.5 + last.astype(jnp.float32)) * contract(ends, ends, ((0,), (0,)), HIGH)
        wcross[...] = contract(ends, lead, ((0,), (0,)), HIGH)

    own_copy.wait()
    own_extra.wait()
    x_extra.wait_recv()

    @pl.when(gets_z)
    def _():
        z_extra.wait_recv()

    @pl.when((h == 1) & has_next)
    def _():
        d_extra.wait_recv()

    @pl.when((h == 0) & jnp.logical_not(has_next))
    def _():
        ext[pl.ds(9, 3), pl.ds(HALF, 8), :] = jnp.zeros((3, 8, UNIT), jnp.float32)

    @pl.when((h == 1) & jnp.logical_not(has_prev))
    def _():
        ext[pl.ds(0, 4), pl.ds(HALF, 8), :] = jnp.zeros((4, 8, UNIT), jnp.float32)

    @pl.when((h == 1) & jnp.logical_not(has_next))
    def _():
        ext[pl.ds(11, 1), pl.ds(HALF, 8), :] = jnp.zeros((1, 8, UNIT), jnp.float32)

    def load(c):
        def unit(t, base):
            e = base + t
            prepare(ext[e + 1, pl.ds(pl.multiple_of(c * UNIT, UNIT), UNIT + 8), :],
                    pl.multiple_of(e * UNIT, UNIT), left, right, after)
            return base
        lax.fori_loop(0, 4, unit, 7 * h, unroll=True)
        x_copy(c).wait_recv()

        @pl.when(gets_z)
        def _():
            z_copy(c).wait_recv()
        lax.fori_loop(0, 7, unit, 4 * (1 - h), unroll=True)

    def gram_lags():
        def lag(p, carry):
            a = h * (3 - p) * UNIT
            acc[p] += product(left, a, right, a + p * UNIT, 8 * UNIT)
            return carry
        lax.fori_loop(0, LAGS, lag, 0, unroll=True)

    def cross_lags():
        def lag(p, carry):
            a = h * (3 - p) * UNIT
            b = a + p * UNIT
            acc[LAGS + p] += product(left, a, after, b, 8 * UNIT)
            acc[2 * LAGS + p] += product(left, b, after, a, 8 * UNIT)
            return carry
        lax.fori_loop(0, LAGS, lag, 0)

    def chunk(step, carry):
        load(CHUNKS - 1 - step)
        gram_lags()
        cross_lags()
        return carry
    lax.fori_loop(0, CHUNKS - 1, chunk, 0)
    load(0)
    gram_lags()

    def term(n, k, l):
        if n < len(GRAM):
            return quarters(acc[l - k])
        return quarters(acc[LAGS + l - k] if l >= k else acc[2 * LAGS + k - l])

    blocks = GRAM + CROSS
    half = len(reduce_refs) // 2
    peers = (lambda d: core_peer, plane_peer, line_peer)
    gram, cross = (
        Total(remote, core, place, q, plane, pairs, piece, peers, (refs[0], out) + refs[1:])
        for piece, out, refs in zip(pieces, (gram_out, cross_out), (reduce_refs[:half], reduce_refs[half:])))

    def gather(total, numbers):
        @pl.when(jnp.logical_not(edge))
        def _():
            for m in range(-LAGS + 1, LAGS):
                which = [n for n in numbers if blocks[n][1] - blocks[n][0] == m]
                if which:
                    value = term(which[0], *blocks[which[0]])
                    for n in which:
                        total.buf[pl.ds((n - numbers[0]) * UNIT, UNIT), :] = value

        @pl.when(edge)
        def _():
            last = jnp.where(at > 0, 1, 0).astype(jnp.float32)
            for n in numbers:
                k, l = blocks[n]
                m = l - k
                value = term(n, k, l)
                less, ends = (dgram, wgram) if n < len(GRAM) else (dcross, wcross)
                for i in range(max(0, -m), min(2, 2 - m) + 1):
                    value = value - less[3 * i + i + m] * ((1.0 - last) if i < k else last)
                value = value - ends[pl.ds(k * UNIT, UNIT), pl.ds(l * UNIT, UNIT)]
                total.buf[pl.ds((n - numbers[0]) * UNIT, UNIT), :] = value
        used, size = len(numbers) * UNIT, total.buf.shape[0]
        if size > used:
            total.buf[pl.ds(used, size - used), :] = jnp.zeros((size - used, UNIT), jnp.float32)

    gather(gram, list(range(len(GRAM))))
    gram.send(0)
    gram.add(0)
    gram.send(1)
    cross_lags()
    gather(cross, list(range(len(GRAM), NB)))
    cross.send(0)
    cross.add(0)
    gram.add(1)
    gram.send(2)
    cross.send(1)
    gram.add(2)
    gram.share(2)
    cross.add(1)
    cross.send(2)
    gram.wait()
    gram.share(1)
    cross.add(2)
    cross.share(2)
    gram.wait()
    gram.share(0)
    cross.wait()
    cross.share(1)
    gram.wait()

    solve = Solve(scale, gram_out, cross_out, tri, op, work, mid, inverses)
    solve.load()

    solve.step(0)
    solve.invert(0)
    cross.wait()
    cross.share(0)
    solve.step(1)
    solve.invert(1)
    cross.wait()
    solve.second_half()

    x_extra.wait_send()
    for c in range(CHUNKS):
        x_copy(c).wait_send()

    @pl.when(sends_z)
    def _():
        z_extra.wait_send()
        for c in range(CHUNKS):
            z_copy(c).wait_send()

    @pl.when((h == 0) & has_prev)
    def _():
        d_extra.wait_send()


def on_device(record):
    count, comps = record.shape
    groups, spans = lax.axis_size("grp"), lax.axis_size("span")
    devices = groups * spans
    lead = (LAGS - 1) * DELAY + 1
    last_row = count * devices - lead
    pairs = spans // 2
    pieces = [-(-n * UNIT // (devices * 8)) * 8 for n in (len(GRAM), len(CROSS))]
    dma = pltpu.SemaphoreType.DMA
    f32, bf16 = jnp.float32, jnp.bfloat16
    vmem = pl.BlockSpec(memory_space=pltpu.VMEM)
    size = LAGS * comps
    return pl.pallas_call(
        functools.partial(whole_kernel, groups, spans, pieces, 1.0 / last_row),
        out_shape=(jax.ShapeDtypeStruct((size, size), f32),) * 2,
        in_specs=[pl.BlockSpec(memory_space=pl.ANY)], out_specs=(vmem, vmem),
        scratch_shapes=[
            *(pltpu.VMEM((piece * devices, UNIT), f32) for piece in pieces),
            *(pltpu.VMEM((size, size), f32),) * 3,
            pltpu.VMEM((12, HALF + 8, UNIT), f32),
            pltpu.VMEM((LAGS + 1, DELAY, UNIT), f32),
            pltpu.VMEM((2 * UNIT, 11 * UNIT), bf16),
            pltpu.VMEM((11 * UNIT, 2 * UNIT), bf16),
            pltpu.VMEM((11 * UNIT, 2 * UNIT), bf16),
            pltpu.VMEM((3 * LAGS, 2 * UNIT, 2 * UNIT), f32),
            pltpu.VMEM((2 * UNIT, 3 * DELAY), bf16),
            pltpu.VMEM((3 * DELAY, 2 * UNIT), bf16),
            pltpu.VMEM((3 * DELAY, 2 * UNIT), bf16),
            pltpu.VMEM((9, UNIT, UNIT), f32),
            pltpu.VMEM((9, UNIT, UNIT), f32),
            pltpu.VMEM((LAGS * UNIT, LAGS * UNIT), f32),
            pltpu.VMEM((LAGS * UNIT, LAGS * UNIT), f32),
            dma((3,)), dma((CHUNKS,)), dma((CHUNKS,)), dma((CHUNKS,)), dma((CHUNKS,)), dma((3,)), dma((3,)),
            *(ref for piece in pieces for ref in (
                pltpu.VMEM((piece * devices, UNIT), f32),
                pltpu.VMEM((1, piece * devices // 2, UNIT), f32),
                pltpu.VMEM((groups - 1, pairs * piece, UNIT), f32),
                pltpu.VMEM((pairs - 1, piece, UNIT), f32),
                *(dma((3, max(groups, pairs) - 1)),) * 4)),
        ],
        compiler_params=pltpu.CompilerParams(
            collective_id=0, has_side_effects=True, vmem_limit_bytes=56 << 20),
    )(record.reshape(LAGS, DELAY, comps))


def solution(mesh):
    placed = (P(AXES, None),)
    return jax.shard_map(
        on_device, mesh=mesh, in_specs=placed, out_specs=(P(), P()), check_vma=False
    )
```

```python
import functools

import jax
import jax.numpy as jnp
from jax import lax
from jax.experimental import pallas as pl
from jax.experimental.pallas import tpu as pltpu
from jax.sharding import PartitionSpec as P

LAGS = 4
DELAY = 1024
AXES = ("grp", "span")
HIGH = lax.Precision.HIGHEST
MESH = pl.DeviceIdType.MESH
UNIT = 128
HALF = DELAY // 2
CHUNKS = HALF // UNIT
GRAM = [(k, l) for k in range(LAGS) for l in range(k, LAGS)]
CROSS = [(k, l) for k in range(LAGS) for l in range(LAGS)]
NB = len(GRAM) + len(CROSS)


def contract(left, right, dims, precision=None):
    return lax.dot_general(
        left, right, (dims, ((), ())), precision=precision,
        preferred_element_type=jnp.float32,
    )


def factor(block):
    n = block.shape[0]
    groups = n // 8
    lane = lax.broadcasted_iota(jnp.int32, (8, n), 1)
    sub = lax.broadcasted_iota(jnp.int32, (8, n), 0)
    a = [block[8 * g:8 * g + 8, :] for g in range(groups)]
    b = [jnp.where(lane == sub + 8 * g, 1.0, 0.0) for g in range(groups)]

    def column(x, k):
        return jnp.broadcast_to(x[:, k:k + 1], (8, n))

    def line(x, i):
        return jnp.broadcast_to(x[i:i + 1, :], (8, n))

    def total(terms):
        while len(terms) > 2:
            terms = [terms[0] + terms[1]] + terms[2:] if len(terms) % 2 else [
                terms[i] + terms[i + 1] for i in range(0, len(terms), 2)]
        return terms[0] + terms[1]

    def stack(rows):
        value = rows[0]
        for i in range(1, 8):
            value = jnp.where(sub == i, rows[i], value)
        return value

    for g in range(groups):
        cols = [column(a[g], 8 * g + j) for j in range(8)]
        s = [[line(cols[j], i) for j in range(i + 1)] for i in range(8)]
        rows = [line(a[g], i) for i in range(8)]
        lines = [line(b[g], i) for i in range(8)]
        inverse, outs, others = [], [], []
        for r in range(8):
            inverse.append(1.0 / s[r][r])
            outs.append(rows[r])
            others.append(lines[r])
            pivot = [s[j][r] for j in range(8)]
            s[r][r + 1:] = pivot[r + 1:]
            for i in range(8):
                if i == r:
                    continue
                f = s[i][r] * inverse[r]
                for j in range(r + 1, i + 1 if i > r else 8):
                    s[i][j] = s[i][j] - f * pivot[j]
                rows[i] = rows[i] - f * rows[r]
                lines[i] = lines[i] - f * lines[r]
        scale = lax.rsqrt(stack([s[r][r] for r in range(8)]))
        left = [rows[r] * inverse[r] for r in range(8)]
        right = [lines[r] * inverse[r] for r in range(8)]
        for h in range(g + 1, groups):
            c = [column(a[h], 8 * g + j) for j in range(8)]
            a[h] = a[h] - total([c[j] * left[j] for j in reversed(range(8))])
            b[h] = b[h] - total([c[j] * right[j] for j in reversed(range(8))])
        a[g] = jnp.where(lane >= sub + 8 * g, stack(outs) * scale, 0.0)
        b[g] = stack(others) * scale
    return jnp.concatenate(a, 0), jnp.concatenate(b, 0)


class Solve:
    def __init__(self, scale, gram, cross, tri, op, work, mid, inverse):
        self.scale, self.gram, self.cross, self.tri, self.op = scale, gram, cross, tri, op
        self.work, self.mid, self.inverse = work, mid, inverse

    def load(self):
        for n, (i, j) in enumerate(GRAM):
            self.work[cut(i), cut(j)] = self.gram[cut(n), :] * self.scale
        self.inverse[...] = jnp.zeros(self.inverse.shape, jnp.float32)

    def load_cross(self):
        for n, (i, j) in enumerate(CROSS):
            self.mid[cut(i), cut(j)] = self.cross[cut(n), :] * self.scale

    def step(self, k):
        work, rest = self.work, LAGS - k - 1
        upper, inverse = factor(work[cut(k), cut(k)])
        work[cut(k), cut(k)] = upper
        self.inverse[cut(k), cut(k)] = inverse
        if rest:
            work[cut(k), cut(k + 1, rest)] = contract(
                inverse, work[cut(k), cut(k + 1, rest)], ((1,), (0,)), HIGH)
        for j in range(k + 1, LAGS):
            to = (cut(j), cut(j, LAGS - j))
            work[to] = work[to] - contract(work[cut(k), cut(j)], work[cut(k), to[1]], ((0,), (0,)), HIGH)

    def invert(self, k):
        inverse = self.inverse
        if k:
            inverse[cut(k), cut(0, k)] = contract(
                inverse[cut(k), cut(k)], inverse[cut(k), cut(0, k)], ((1,), (0,)), HIGH)
        if k < LAGS - 1:
            to = (cut(k + 1, LAGS - k - 1), cut(0, k + 1))
            inverse[to] = inverse[to] - contract(
                self.work[cut(k), to[0]], inverse[cut(k), to[1]], ((0,), (0,)), HIGH)

    def apply(self, k):
        mid = self.mid
        mid[cut(k), :] = contract(self.inverse[cut(k), cut(k)], mid[cut(k), :], ((1,), (0,)), HIGH)
        if k < LAGS - 1:
            below = cut(k + 1, LAGS - k - 1)
            mid[below, :] = mid[below, :] - contract(
                self.work[cut(k), below], mid[cut(k), :], ((0,), (0,)), HIGH)

    def operate(self, rows, cols, depth):
        self.op[rows, cols] = contract(
            self.mid[rows, cut(0, depth)], self.inverse[cols, cut(0, depth)], ((1,), (1,)), HIGH)

    def triangle(self):
        for i in range(LAGS):
            self.tri[cut(i), cut(i, LAGS - i)] = self.work[cut(i), cut(i, LAGS - i)]
            if i:
                self.tri[cut(i), cut(0, i)] = jnp.zeros((UNIT, i * UNIT), jnp.float32)

    def second_half(self):
        self.load_cross()
        self.step(2)
        self.apply(0)
        self.apply(1)
        self.step(3)
        self.apply(2)
        self.invert(2)
        self.operate(cut(0, 3), cut(0, 3), 3)
        self.apply(3)
        self.invert(3)
        self.operate(cut(0, 3), cut(3), 4)
        self.operate(cut(3), cut(0, 4), 4)
        self.triangle()


def cut(n, count=1):
    return pl.ds(n * UNIT, count * UNIT)


def halves(x):
    spread = x * 65537.0
    high = spread - (spread - x)
    return high.astype(jnp.bfloat16), (x - high).astype(jnp.bfloat16)


def quarters(x):
    n = x.shape[0] // 2
    return (x[:n, :n] + x[:n, n:]) + (x[n:, :n] + x[n:, n:])


def prepare(window, at, left, right, after):
    cols = pl.ds(at, UNIT)
    rows = window[:UNIT]
    high, low = halves(rows)
    right[cols, pl.ds(0, UNIT)] = high
    right[cols, pl.ds(UNIT, UNIT)] = low
    high, low = halves(rows.T)
    left[pl.ds(0, UNIT), cols] = high
    left[pl.ds(UNIT, UNIT), cols] = low
    high, low = halves(pltpu.roll(window, window.shape[0] - 1, 0)[:UNIT])
    after[cols, pl.ds(0, UNIT)] = high
    after[cols, pl.ds(UNIT, UNIT)] = low


def product(left, lcol, right, rrow, depth):
    lcol = pl.multiple_of(lcol, UNIT)
    rrow = pl.multiple_of(rrow, UNIT)
    return jnp.dot(left[:, pl.ds(lcol, depth)], right[pl.ds(rrow, depth), :],
                   preferred_element_type=jnp.float32)


class Total:
    def __init__(self, remote, core, place, q, plane, pairs, piece, peers, refs):
        self.buf, self.out, self.slots = refs[0], refs[1], refs[2:5]
        self.sems = refs[5:]
        self.remote, self.piece = remote, piece
        self.sizes = (plane * pairs * piece, pairs * piece, piece)
        self.index, self.counts, self.peers = (core, place, q), (2, plane, pairs), peers
        self.base = [0]
        for size, index in zip(self.sizes, self.index):
            self.base.append(self.base[-1] + index * size)
        self.copies = []

    def rows(self, level, n):
        size = self.sizes[level]
        return pl.ds(pl.multiple_of(self.base[level] + n * size, 8), size)

    def send(self, level):
        self.copies = []
        for d in range(1, self.counts[level]):
            there = (self.index[level] + d) % self.counts[level]
            self.copies.append(self.remote(
                self.buf.at[self.rows(level, there)], self.slots[level].at[d - 1],
                self.sems[0].at[level, d - 1], self.sems[1].at[level, d - 1], self.peers[level](d)))
            self.copies[-1].start()

    def add(self, level):
        for copy in self.copies:
            copy.wait()
        mine = self.rows(level, self.index[level])
        value = self.buf[mine, :]
        for d in range(1, self.counts[level]):
            value = value + self.slots[level][d - 1]
        if level == 2:
            self.out[mine, :] = value
        else:
            self.buf[mine, :] = value

    def share(self, level, start=True):
        mine = self.out.at[self.rows(level, self.index[level])]
        self.copies = []
        for d in range(1, self.counts[level]):
            self.copies.append(self.remote(
                mine, mine, self.sems[2].at[level, d - 1], self.sems[3].at[level, d - 1], self.peers[level](d)))
        if start:
            self.start()

    def start(self):
        for copy in self.copies:
            copy.start()

    def wait(self):
        for copy in self.copies:
            copy.wait()


def whole_kernel(groups, spans, pieces, scale, rec, tri, op, gram_out, cross_out, work, mid, inverses, ext, own, left, right, after, acc,
                eleft, eright, eafter, dgram, dcross, wgram, wcross,
                local_sem, xs, xr, zs, zr, es, er, *reduce_refs):
    grp, span = lax.axis_index("grp"), lax.axis_index("span")
    pairs = spans // 2
    h, q = span % 2, span // 2
    core, y = grp % 2, grp // 2
    plane, place = groups, y * 2 + h
    at, count = grp * pairs + q, groups * pairs
    has_prev, has_next = at > 0, at < count - 1

    def device(pair, side):
        pair = (pair + count) % count
        return (pair // pairs, (pair % pairs) * 2 + side)

    def plane_peer(d):
        there = (place + d) % plane
        return ((there // 2) * 2 + core, q * 2 + there % 2)

    def line_peer(d):
        return (grp, ((q + d) % pairs) * 2 + h)

    core_peer = (y * 2 + 1 - core, span)
    partner = (grp, q * 2 + 1 - h)
    z_to = device(at - 1 + 2 * h, h)
    sends_z = jnp.where(h == 0, at, count - 1 - at) > 0
    gets_z = jnp.where(h == 0, count - 1 - at, at) > 0

    own_copy = pltpu.make_async_copy(
        rec.at[:, pl.ds(h * HALF, HALF), :], ext.at[pl.ds(1 + 7 * h, 4), pl.ds(0, HALF), :], local_sem.at[0])
    own_extra = pltpu.make_async_copy(
        rec.at[:, pl.ds((1 - h) * HALF, 8), :], ext.at[pl.ds(1 + 6 * h, 4), pl.ds(HALF, 8), :], local_sem.at[1])
    own_copy.start()
    own_extra.start()
    edge = (at * 2 + h == 0) | (at * 2 + h == 2 * count - 1)
    full_copy = pltpu.make_async_copy(rec, own.at[pl.ds(0, LAGS)], local_sem.at[2])

    @pl.when(edge)
    def _():
        full_copy.start()

    barrier = pltpu.get_barrier_semaphore()

    def greet(to):
        pl.semaphore_signal(barrier, inc=1, device_id=to, device_id_type=MESH)

    greet(core_peer)
    for d in range(1, plane):
        greet(plane_peer(d))
    for d in range(1, pairs):
        greet(line_peer(d))

    @pl.when(has_prev)
    def _():
        greet(device(at - 1, h))

    @pl.when(has_next)
    def _():
        greet(device(at + 1, h))

    @pl.when((h == 0) & has_prev)
    def _():
        greet(device(at - 1, 1))

    @pl.when((h == 1) & has_next)
    def _():
        greet(device(at + 1, 0))

    pl.semaphore_wait(
        barrier, plane + pairs - 1
        + jnp.where(has_prev, 1, 0) + jnp.where(has_next, 1, 0)
        + jnp.where((h == 0) & has_prev, 1, 0) + jnp.where((h == 1) & has_next, 1, 0))

    def remote(src, dst, send, recv, to):
        return pltpu.make_async_remote_copy(
            src_ref=src, dst_ref=dst, send_sem=send, recv_sem=recv, device_id=to, device_id_type=MESH)

    def x_copy(c):
        return remote(
            rec.at[:, pl.ds((1 - h) * HALF + c * UNIT, UNIT), :],
            ext.at[pl.ds(4 + h, 4), pl.ds(c * UNIT, UNIT), :], xs.at[c], xr.at[c], partner)

    def z_copy(c):
        return remote(
            rec.at[pl.ds(h, 3), pl.ds(h * HALF + c * UNIT, UNIT), :],
            ext.at[pl.ds(9 - 8 * h, 3), pl.ds(c * UNIT, UNIT), :], zs.at[c], zr.at[c], z_to)

    x_extra = remote(
        rec.at[:, pl.ds(h * HALF, 8), :], ext.at[pl.ds(3 + 2 * h, 4), pl.ds(HALF, 8), :],
        es.at[0], er.at[0], partner)
    z_extra = remote(
        rec.at[pl.ds(h, 3), pl.ds((1 - h) * HALF, 8), :], ext.at[pl.ds(9 - 9 * h, 3), pl.ds(HALF, 8), :],
        es.at[1], er.at[1], z_to)
    d_extra = remote(
        rec.at[pl.ds(0, 1), pl.ds(0, 8), :], ext.at[pl.ds(11, 1), pl.ds(HALF, 8), :],
        es.at[2], er.at[2], device(at - 1, 1))

    x_extra.start()
    for c in reversed(range(CHUNKS)):
        x_copy(c).start()

    @pl.when(sends_z)
    def _():
        z_extra.start()
        for c in reversed(range(CHUNKS)):
            z_copy(c).start()

    @pl.when((h == 0) & has_prev)
    def _():
        d_extra.start()

    @pl.when(jnp.logical_not(gets_z))
    def _():
        ext[pl.ds(9 - 8 * h, 3), pl.ds(0, HALF), :] = jnp.zeros((3, HALF, UNIT), jnp.float32)

    acc[...] = jnp.zeros(acc.shape, jnp.float32)

    @pl.when(edge)
    def _():
        last = jnp.where(at > 0, 1, 0)
        own[LAGS, pl.ds(0, 8), :] = jnp.zeros((8, UNIT), jnp.float32)
        full_copy.wait()
        parts = DELAY // UNIT

        def unit(t, carry):
            block, row = t // parts, (t % parts) * UNIT
            rows = own[last + block, pl.ds(pl.multiple_of(row, UNIT), UNIT), :]
            more = t + 1
            tail = own[last + more // parts, pl.ds(pl.multiple_of((more % parts) * UNIT, UNIT), 8), :]
            prepare(jnp.concatenate([rows, tail], 0), pl.multiple_of(t * UNIT, UNIT), eleft, eright, eafter)
            return carry
        lax.fori_loop(0, 3 * parts, unit, 0)

        def excess(t, carry):
            i, j = t // 3, t % 3
            dgram[t] = quarters(product(eleft, i * DELAY, eright, j * DELAY, DELAY))
            dcross[t] = quarters(product(eleft, i * DELAY, eafter, j * DELAY, DELAY))
            return carry
        lax.fori_loop(0, 9, excess, 0)

        sub = lax.broadcasted_iota(jnp.int32, (8, UNIT), 0)

        def pick(block, start, row):
            rows = jnp.where(sub == row, own[block, pl.ds(pl.multiple_of(start, 8), 8), :], 0.0)
            line = jnp.sum(rows, axis=0, keepdims=True)
            return jnp.where(sub == 0, jnp.broadcast_to(line, (8, UNIT)), 0.0)
        ends = jnp.concatenate([pick(k, last * (DELAY - 8), last * 7) for k in range(LAGS)], 1)
        lead = jnp.concatenate([pick(l + 1, 0, 0) for l in range(LAGS)], 1)
        lead = lead * last.astype(jnp.float32)
        wgram[...] = (0.5 + last.astype(jnp.float32)) * contract(ends, ends, ((0,), (0,)), HIGH)
        wcross[...] = contract(ends, lead, ((0,), (0,)), HIGH)

    own_copy.wait()
    own_extra.wait()
    x_extra.wait_recv()

    @pl.when(gets_z)
    def _():
        z_extra.wait_recv()

    @pl.when((h == 1) & has_next)
    def _():
        d_extra.wait_recv()

    @pl.when((h == 0) & jnp.logical_not(has_next))
    def _():
        ext[pl.ds(9, 3), pl.ds(HALF, 8), :] = jnp.zeros((3, 8, UNIT), jnp.float32)

    @pl.when((h == 1) & jnp.logical_not(has_prev))
    def _():
        ext[pl.ds(0, 4), pl.ds(HALF, 8), :] = jnp.zeros((4, 8, UNIT), jnp.float32)

    @pl.when((h == 1) & jnp.logical_not(has_next))
    def _():
        ext[pl.ds(11, 1), pl.ds(HALF, 8), :] = jnp.zeros((1, 8, UNIT), jnp.float32)

    def load(c):
        def unit(t, base):
            e = base + t
            prepare(ext[e + 1, pl.ds(pl.multiple_of(c * UNIT, UNIT), UNIT + 8), :],
                    pl.multiple_of(e * UNIT, UNIT), left, right, after)
            return base
        lax.fori_loop(0, 4, unit, 7 * h, unroll=True)
        x_copy(c).wait_recv()

        @pl.when(gets_z)
        def _():
            z_copy(c).wait_recv()
        lax.fori_loop(0, 7, unit, 4 * (1 - h), unroll=True)

    def gram_lags():
        def lag(p, carry):
            a = h * (3 - p) * UNIT
            acc[p] += product(left, a, right, a + p * UNIT, 8 * UNIT)
            return carry
        lax.fori_loop(0, LAGS, lag, 0, unroll=True)

    def cross_lags():
        def lag(p, carry):
            a = h * (3 - p) * UNIT
            b = a + p * UNIT
            acc[LAGS + p] += product(left, a, after, b, 8 * UNIT)
            acc[2 * LAGS + p] += product(left, b, after, a, 8 * UNIT)
            return carry
        lax.fori_loop(0, LAGS, lag, 0, unroll=True)

    def chunk(step, carry):
        load(CHUNKS - 1 - step)
        gram_lags()
        cross_lags()
        return carry
    lax.fori_loop(0, CHUNKS - 1, chunk, 0)
    load(0)
    gram_lags()

    def term(n, k, l):
        if n < len(GRAM):
            return quarters(acc[l - k])
        return quarters(acc[LAGS + l - k] if l >= k else acc[2 * LAGS + k - l])

    blocks = GRAM + CROSS
    half = len(reduce_refs) // 2
    peers = (lambda d: core_peer, plane_peer, line_peer)
    gram, cross = (
        Total(remote, core, place, q, plane, pairs, piece, peers, (refs[0], out) + refs[1:])
        for piece, out, refs in zip(pieces, (gram_out, cross_out), (reduce_refs[:half], reduce_refs[half:])))

    def gather(total, numbers):
        @pl.when(jnp.logical_not(edge))
        def _():
            for m in range(-LAGS + 1, LAGS):
                which = [n for n in numbers if blocks[n][1] - blocks[n][0] == m]
                if which:
                    value = term(which[0], *blocks[which[0]])
                    for n in which:
                        total.buf[pl.ds((n - numbers[0]) * UNIT, UNIT), :] = value

        @pl.when(edge)
        def _():
            last = jnp.where(at > 0, 1, 0).astype(jnp.float32)
            for n in numbers:
                k, l = blocks[n]
                m = l - k
                value = term(n, k, l)
                less, ends = (dgram, wgram) if n < len(GRAM) else (dcross, wcross)
                for i in range(max(0, -m), min(2, 2 - m) + 1):
                    value = value - less[3 * i + i + m] * ((1.0 - last) if i < k else last)
                value = value - ends[pl.ds(k * UNIT, UNIT), pl.ds(l * UNIT, UNIT)]
                total.buf[pl.ds((n - numbers[0]) * UNIT, UNIT), :] = value
        used, size = len(numbers) * UNIT, total.buf.shape[0]
        if size > used:
            total.buf[pl.ds(used, size - used), :] = jnp.zeros((size - used, UNIT), jnp.float32)

    gather(gram, list(range(len(GRAM))))
    gram.send(0)
    gram.add(0)
    gram.send(1)
    cross_lags()
    gather(cross, list(range(len(GRAM), NB)))
    cross.send(0)
    cross.add(0)
    gram.add(1)
    gram.send(2)
    cross.send(1)
    gram.add(2)
    gram.share(2)
    cross.add(1)
    cross.send(2)
    gram.wait()
    gram.share(1)
    cross.add(2)
    cross.share(2)
    gram.wait()
    gram.share(0)
    cross.wait()
    cross.share(1)
    gram.wait()

    solve = Solve(scale, gram_out, cross_out, tri, op, work, mid, inverses)
    solve.load()

    solve.step(0)
    solve.invert(0)
    cross.wait()
    cross.share(0)
    solve.step(1)
    solve.invert(1)
    cross.wait()
    solve.second_half()

    x_extra.wait_send()
    for c in range(CHUNKS):
        x_copy(c).wait_send()

    @pl.when(sends_z)
    def _():
        z_extra.wait_send()
        for c in range(CHUNKS):
            z_copy(c).wait_send()

    @pl.when((h == 0) & has_prev)
    def _():
        d_extra.wait_send()


def on_device(record):
    count, comps = record.shape
    groups, spans = lax.axis_size("grp"), lax.axis_size("span")
    devices = groups * spans
    lead = (LAGS - 1) * DELAY + 1
    last_row = count * devices - lead
    pairs = spans // 2
    pieces = [-(-n * UNIT // (devices * 8)) * 8 for n in (len(GRAM), len(CROSS))]
    dma = pltpu.SemaphoreType.DMA
    f32, bf16 = jnp.float32, jnp.bfloat16
    vmem = pl.BlockSpec(memory_space=pltpu.VMEM)
    size = LAGS * comps
    return pl.pallas_call(
        functools.partial(whole_kernel, groups, spans, pieces, 1.0 / last_row),
        out_shape=(jax.ShapeDtypeStruct((size, size), f32),) * 2,
        in_specs=[pl.BlockSpec(memory_space=pl.ANY)], out_specs=(vmem, vmem),
        scratch_shapes=[
            *(pltpu.VMEM((piece * devices, UNIT), f32) for piece in pieces),
            *(pltpu.VMEM((size, size), f32),) * 3,
            pltpu.VMEM((12, HALF + 8, UNIT), f32),
            pltpu.VMEM((LAGS + 1, DELAY, UNIT), f32),
            pltpu.VMEM((2 * UNIT, 11 * UNIT), bf16),
            pltpu.VMEM((11 * UNIT, 2 * UNIT), bf16),
            pltpu.VMEM((11 * UNIT, 2 * UNIT), bf16),
            pltpu.VMEM((3 * LAGS, 2 * UNIT, 2 * UNIT), f32),
            pltpu.VMEM((2 * UNIT, 3 * DELAY), bf16),
            pltpu.VMEM((3 * DELAY, 2 * UNIT), bf16),
            pltpu.VMEM((3 * DELAY, 2 * UNIT), bf16),
            pltpu.VMEM((9, UNIT, UNIT), f32),
            pltpu.VMEM((9, UNIT, UNIT), f32),
            pltpu.VMEM((LAGS * UNIT, LAGS * UNIT), f32),
            pltpu.VMEM((LAGS * UNIT, LAGS * UNIT), f32),
            dma((3,)), dma((CHUNKS,)), dma((CHUNKS,)), dma((CHUNKS,)), dma((CHUNKS,)), dma((3,)), dma((3,)),
            *(ref for piece in pieces for ref in (
                pltpu.VMEM((piece * devices, UNIT), f32),
                pltpu.VMEM((1, piece * devices // 2, UNIT), f32),
                pltpu.VMEM((groups - 1, pairs * piece, UNIT), f32),
                pltpu.VMEM((pairs - 1, piece, UNIT), f32),
                *(dma((3, max(groups, pairs) - 1)),) * 4)),
        ],
        compiler_params=pltpu.CompilerParams(
            collective_id=0, has_side_effects=True, vmem_limit_bytes=56 << 20),
    )(record.reshape(LAGS, DELAY, comps))


def solution(mesh):
    placed = (P(AXES, None),)
    return jax.shard_map(
        on_device, mesh=mesh, in_specs=placed, out_specs=(P(), P()), check_vma=False
    )
```
